32 devices in a mesh: space: 16 (over z, y, core), filt: 2 (over x).
Axes of the slice: x: 2, y: 2, z: 4, core: 2. Of those that a mesh axis runs over, the one named last changes fastest.
Arguments:
- volume: bfloat16 [64, 32, 4, 256], P(None, 'space', 'filt'), may hold values from -6 to 6
- first_weight: bfloat16 [27, 64, 64], replicated, may hold values from -0.15625 to 0.15625
- second_weight: bfloat16 [27, 128, 64], P(None, 'filt'), may hold values from -0.15625 to 0.15625
- cotangent: bfloat16 [128, 16, 2, 128], P('filt', 'space'), may hold values from -24 to 24
Outputs:
- features: bfloat16 [128, 16, 2, 128], P('filt', 'space')
- volume_grad: bfloat16 [64, 32, 4, 256], P(None, 'space', 'filt')
- first_grad: float32 [27, 64, 64], replicated
- second_grad: float32 [27, 128, 64], P(None, 'filt')
The draws below stay inside these ranges and needn't reach their ends.
All inputs are finite; a program needn't handle non-finite values.
Results may differ from the reference program's by a relative error of at most 0.019.
Values may be sent and summed in bfloat16 or wider, within the bound.
No kernel may reach another device: no remote copies, remote signals or barrier semaphores. Data moves between devices by JAX's collectives and lax.ppermute only.
A program may use at most 64 MiB of HBM per device.

```python
import jax
import jax.numpy as jnp
from jax import lax

C1 = 64
C2 = 128
Z3 = 128
X3 = 16
Y3 = 2
X2 = 32
Y2 = 4
Z2 = 256
N_FILT = 2


def shard_levels(own_key, dims, cuts, smallest, largest):
    def one(position, shards_of):
        heights = jax.random.uniform(jax.random.fold_in(jax.random.fold_in(own_key, 6), position), (shards_of,), jnp.float32, smallest / len(cuts), largest / len(cuts))
        return jnp.repeat(jnp.exp(heights), dims[position] // shards_of).reshape((-1,) + (1,) * (len(dims) - position - 1))

    factor_of = one(*cuts[0])
    for cut in cuts[1:]:
        factor_of = factor_of * one(*cut)
    return factor_of


def noise(stream_key, dims, scale, most, shards=(), dtype=jnp.bfloat16):
    values = scale * jax.random.normal(stream_key, dims, jnp.float32)
    if shards:
        values = values * shard_levels(stream_key, dims, shards, -0.22, 0.18)
    return jnp.clip(values, -most, most).astype(dtype)


def setup_inputs(seed: int = 0) -> dict:
    splits = jax.random.split(jax.random.key(seed), 5)
    return {
        "volume": noise(splits[0], (C1, X2, Y2, Z2), 1.0, 6.0, ((1, 16), (2, 2))),
        "first_weight": noise(splits[1], (27, C1, C1), (27 * C1) ** -0.5, 0.15625),
        "second_weight": noise(splits[2], (27, C2, C1), (27 * C1) ** -0.5, 0.15625, ((1, 2),)),
        "cotangent": noise(splits[3], (C2, X3, Y3, Z3), 4.0, 24.0, ((0, 2), (1, 16))),
    }


def silu_slope(values):
    sigmoid_part = jax.nn.sigmoid(values)
    return sigmoid_part * (1.0 + values * (1.0 - sigmoid_part))


def pad_all(volume_field):
    return jnp.pad(volume_field, ((0, 0), (1, 1), (1, 1), (1, 1)))


def window(padded, offset_x, offset_y, offset_z, extents):
    extent_x, extent_y, extent_z = extents
    section = lax.slice(padded, (0, offset_x, offset_y, offset_z), (padded.shape[0], offset_x + extent_x, offset_y + extent_y, offset_z + extent_z))
    return section.reshape(padded.shape[0], extent_x * extent_y * extent_z)


def conv_forward(padded, weight, extents):
    outputs, inputs = weight.shape[1], weight.shape[2]
    running = jnp.zeros((outputs, extents[0] * extents[1] * extents[2]), jnp.float32)
    for offset_x in range(3):
        for offset_y in range(3):
            tap_base = offset_x * 9 + offset_y * 3
            stacked = jnp.concatenate([window(padded, offset_x, offset_y, offset_z, extents) for offset_z in range(3)], axis=0)
            matrices = jnp.transpose(weight[tap_base:tap_base + 3], (1, 0, 2)).reshape(outputs, 3 * inputs)
            running = running + jnp.dot(matrices, stacked, preferred_element_type=jnp.float32)
    return running


def conv_transpose(padded, weight, extents):
    outputs, inputs = weight.shape[1], weight.shape[2]
    running = jnp.zeros((inputs, extents[0] * extents[1] * extents[2]), jnp.float32)
    for offset_x in range(3):
        for offset_y in range(3):
            tap_base = offset_x * 9 + offset_y * 3
            stacked = jnp.concatenate([window(padded, offset_x, offset_y, offset_z, extents) for offset_z in range(3)], axis=0)
            tap_block = weight[24 - tap_base:27 - tap_base][::-1]
            matrices = jnp.transpose(tap_block, (2, 0, 1)).reshape(inputs, 3 * outputs)
            running = running + jnp.dot(matrices, stacked, preferred_element_type=jnp.float32)
    return running


def conv_weights(grad_rows, padded, extents):
    outputs, inputs = grad_rows.shape[0], padded.shape[0]
    blocks = []
    for offset_x in range(3):
        for offset_y in range(3):
            stacked = jnp.concatenate([window(padded, offset_x, offset_y, offset_z, extents) for offset_z in range(3)], axis=0)
            section = lax.dot_general(grad_rows, stacked, (((1,), (1,)), ((), ())), preferred_element_type=jnp.float32)
            blocks.append(jnp.transpose(section.reshape(outputs, 3, inputs), (1, 0, 2)))
    return jnp.concatenate(blocks, axis=0)


def pool_cells(hidden):
    channels, size_x, size_y, size_z = hidden.shape
    pair_table = (jnp.arange(size_z)[:, None] // 2 == jnp.arange(size_z // 2)[None, :]).astype(jnp.bfloat16)
    depth_sums = jnp.dot(hidden.reshape(-1, size_z), pair_table, preferred_element_type=jnp.float32)
    depth_sums = depth_sums.reshape(channels, size_x // 2, 2, size_y // 2, 2, size_z // 2)
    return (0.125 * depth_sums.sum(axis=(2, 4))).astype(jnp.bfloat16)


def spread_cells(grad_field):
    scaled = 0.125 * grad_field
    scaled = jnp.repeat(scaled, 2, axis=1)
    scaled = jnp.repeat(scaled, 2, axis=2)
    return jnp.repeat(scaled, 2, axis=3)


def reference(volume, first_weight, second_weight, cotangent):
    channels = volume.shape[0]
    fine_shape = volume.shape[1:]
    padded_in = pad_all(volume)
    first_pre = conv_forward(padded_in, first_weight, fine_shape)
    hidden = jax.nn.silu(first_pre).astype(jnp.bfloat16).reshape((channels,) + fine_shape)
    pooled = pool_cells(hidden)
    slab_shape = pooled.shape[1:]
    padded_pool = pad_all(pooled)
    second_pre = conv_forward(padded_pool, second_weight, slab_shape)
    total_filters = second_weight.shape[1]
    features = jax.nn.silu(second_pre).astype(jnp.bfloat16).reshape((total_filters,) + slab_shape)
    down_grad = (cotangent.reshape(total_filters, -1).astype(jnp.float32) * silu_slope(second_pre)).astype(jnp.bfloat16)
    bottom_scale = 1.0 / (slab_shape[0] * slab_shape[1] * slab_shape[2]) ** 0.5
    second_grad = conv_weights(down_grad, padded_pool, slab_shape) * bottom_scale
    padded_down = pad_all(down_grad.reshape((total_filters,) + slab_shape))
    group_size = total_filters // N_FILT
    pool_grad = jnp.zeros((channels, slab_shape[0] * slab_shape[1] * slab_shape[2]), jnp.float32)
    for group_index in range(N_FILT):
        lower = group_index * group_size
        section = conv_transpose(padded_down[lower:lower + group_size], second_weight[:, lower:lower + group_size], slab_shape)
        pool_grad = pool_grad + lax.optimization_barrier(section.astype(jnp.bfloat16)).astype(jnp.float32)
    hidden_grad = spread_cells(pool_grad.reshape((channels,) + slab_shape))
    first_down = (hidden_grad.reshape(channels, -1) * silu_slope(first_pre)).astype(jnp.bfloat16)
    fine_scale = 1.0 / (fine_shape[0] * fine_shape[1] * fine_shape[2]) ** 0.5
    first_grad = conv_weights(first_down, padded_in, fine_shape) * fine_scale
    padded_back = pad_all(first_down.reshape((channels,) + fine_shape))
    volume_grad = conv_transpose(padded_back, first_weight, fine_shape).astype(jnp.bfloat16).reshape((channels,) + fine_shape)
    return (features, volume_grad, first_grad, second_grad)
```

```python
import functools

import jax
import jax.numpy as jnp
from jax import lax
from jax.experimental import pallas as pl
from jax.experimental.pallas import tpu as pltpu
from jax.sharding import PartitionSpec as P

F32 = jnp.float32
BF16 = jnp.bfloat16
VMEM_LIMIT = 56 * 1024 * 1024


def call(body, outs, scratch=(), name=None):
    return pl.pallas_call(
        body,
        out_shape=outs,
        scratch_shapes=scratch,
        name=name,
        compiler_params=pltpu.CompilerParams(vmem_limit_bytes=VMEM_LIMIT),
    )


def shaped(shape, dtype):
    return jax.ShapeDtypeStruct(shape, dtype)


def dot(lhs, rhs):
    return jnp.dot(lhs, rhs, preferred_element_type=F32)


def dot_cells(lhs, rhs):
    return lax.dot_general(lhs, rhs, (((1,), (1,)), ((), ())), preferred_element_type=F32)


def silu_slope(values):
    part = 1.0 / (1.0 + jnp.exp(-values))
    return part * (1.0 + values * (1.0 - part))


def silu(values):
    return values / (1.0 + jnp.exp(-values))


def stack3(cells, depth):
    count = cells.shape[1]
    lane = lax.broadcasted_iota(jnp.int32, cells.shape, 1) % depth
    wide = cells.astype(F32)
    below = jnp.where(lane == 0, 0.0, pltpu.roll(wide, 1, 1)).astype(BF16)
    above = jnp.where(lane == depth - 1, 0.0, pltpu.roll(wide, count - 1, 1)).astype(BF16)
    return jnp.concatenate([below, cells, above], axis=0)


def shifted_rows(cells, offset, depth):
    if offset == 0:
        return cells
    blank = jnp.zeros((cells.shape[0], depth), cells.dtype)
    if cells.shape[1] == depth:
        return blank
    if offset > 0:
        return jnp.concatenate([cells[:, depth:], blank], axis=1)
    return jnp.concatenate([blank, cells[:, :-depth]], axis=1)


def conv_planes(matrices, stacks, planes, outputs, depth):
    results = [None] * planes
    for place in range(planes + 2):
        first = max(0, place - planes + 1)
        last = min(2, place)
        rows = matrices[first * 3 * outputs : (last + 1) * 3 * outputs, :]
        terms = dot(rows, stacks[place])
        for tap_x in range(first, last + 1):
            for tap_y in range(3):
                begin = ((tap_x - first) * 3 + tap_y) * outputs
                term = shifted_rows(terms[begin : begin + outputs], tap_y - 1, depth)
                target = place - tap_x
                results[target] = term if results[target] is None else results[target] + term
    return results


def weight_planes(acc, grads, stacks, depth):
    planes = len(grads)
    outputs = grads[0].shape[0]
    rows = [
        jnp.concatenate([shifted_rows(grad, 1 - tap_y, depth) for tap_y in range(3)], axis=0)
        for grad in grads
    ]
    for tap_x in range(3):
        total = None
        for plane in range(planes):
            term = dot_cells(rows[plane], stacks[plane + tap_x])
            total = term if total is None else total + term
        acc[tap_x * 3 * outputs : (tap_x + 1) * 3 * outputs, :] = total


def pack(acc, target, base, rows):
    half = rows // 2
    target[base : base + rows, :] = acc[:, :128]
    target[base + rows : base + rows + half, :] = jnp.concatenate(
        [acc[:half, 128:], acc[half:, 128:]], axis=1
    )


def unpack(source, base, rows, out, scale):
    half = rows // 2
    outputs = rows // 9
    for pair in range(9):
        main = source[base + pair * outputs : base + (pair + 1) * outputs, :].astype(F32) * scale
        out[3 * pair] = main[:, :64]
        out[3 * pair + 1] = main[:, 64:]
    for piece in range(0, 9 * outputs, 8):
        row = piece if piece < half else piece - half
        tail = source[base + rows + row : base + rows + row + 8, :].astype(F32) * scale
        side = tail[:, :64] if piece < half else tail[:, 64:]
        out[3 * (piece // outputs) + 2, piece % outputs : piece % outputs + 8, :] = side


def halo_places():
    index = lax.axis_index("space")
    ends = lax.axis_size("space") - 1
    a_right = 1 - index % 2
    inside = jnp.logical_and(index > 0, index < ends)
    return a_right, inside


def ordered_halos(got_a, got_b):
    a_right, inside = halo_places()
    got_b = jnp.where(inside, got_b, jnp.zeros_like(got_b))
    left = jnp.where(a_right == 1, got_b, got_a)
    right = jnp.where(a_right == 1, got_a, got_b)
    return left, right


def swap_tables(count):
    table_a = [(i, i ^ 1) for i in range(count)]
    table_b = [(0, 0)]
    for i in range(1, count - 1, 2):
        table_b += [(i, i + 1), (i + 1, i)]
    table_b.append((count - 1, count - 1))
    return table_a, table_b


def halves(shape):
    return pltpu.VMEM(shape, BF16)


def join_rows(target, place, pieces, brick):
    index = lax.axis_index("filt")
    for slot, piece in enumerate(pieces):
        start = pl.multiple_of((index ^ slot) * brick, brick)
        target[place, :, pl.ds(start, brick)] = piece


def local(space, filt, volume, first_weight, second_weight, cotangent):
    channels, planes, brick_y, depth = volume.shape
    filters = second_weight.shape[1]
    table_a, table_b = swap_tables(space)
    fine_y = brick_y * filt
    low_y = fine_y // 2
    low_depth = depth // 2
    fine_cells = fine_y * depth
    low_cells = low_y * low_depth
    brick = brick_y * depth
    fine_scale = 1.0 / (planes * space * fine_cells) ** 0.5
    low_scale = 1.0 / (planes // 2 * space * low_cells) ** 0.5
    low_planes = planes // 2

    def swap_a(piece):
        return lax.ppermute(piece, "space", table_a)

    def swap_b(piece):
        return lax.ppermute(piece, "space", table_b)

    def both(table, slot):
        return [(i * filt + f, j * filt + (f ^ slot)) for i, j in table for f in range(filt)]

    def across(piece, table, slot):
        return lax.ppermute(piece, ("space", "filt"), both(table, slot))

    place = lax.axis_index("space")
    own_table = [(i, i) for i in range(space)]
    brick_rows = jnp.transpose(volume, (1, 0, 2, 3)).reshape(planes, channels, brick)
    odd = place % 2
    edge_a = jnp.where(odd == 1, brick_rows[0], brick_rows[planes - 1])
    edge_b = jnp.where(odd == 1, brick_rows[planes - 1], brick_rows[0])
    own = [brick_rows] + [across(brick_rows, own_table, slot) for slot in range(1, filt)]
    halo_a = [across(edge_a, table_a, slot) for slot in range(filt)]
    halo_b = [across(edge_b, table_b, slot) for slot in range(filt)]

    first_taps = first_weight.reshape(9, 3, channels, channels)
    first_forward = jnp.transpose(first_taps, (0, 2, 1, 3)).reshape(9 * channels, 3 * channels)
    first_back = jnp.transpose(first_taps[::-1, ::-1], (0, 3, 1, 2)).reshape(
        9 * channels, 3 * channels
    )
    second_taps = second_weight.reshape(9, 3, filters, channels)
    second_forward = jnp.transpose(second_taps, (0, 2, 1, 3)).reshape(9 * filters, 3 * channels)
    second_back = jnp.transpose(second_taps[::-1, ::-1], (0, 3, 1, 2)).reshape(
        9 * channels, 3 * filters
    )
    low_cot = cotangent.reshape(filters, low_cells)

    def first_kernel(*refs):
        own_refs = refs[:filt]
        a_refs = refs[filt : 2 * filt]
        b_refs = refs[2 * filt : 3 * filt]
        matrices, pooled_ref, slope_ref, whole_ref = refs[3 * filt : 3 * filt + 4]
        for plane in range(planes):
            join_rows(whole_ref, 1 + plane, [ref[plane] for ref in own_refs], brick)
        halos = [ordered_halos(a[...], b[...]) for a, b in zip(a_refs, b_refs)]
        join_rows(whole_ref, 0, [pair[0] for pair in halos], brick)
        join_rows(whole_ref, planes + 1, [pair[1] for pair in halos], brick)
        stacks = [stack3(whole_ref[p], depth) for p in range(planes + 2)]
        pre = conv_planes(matrices, stacks, planes, channels, depth)
        hidden = [silu(value).astype(BF16) for value in pre]
        for plane in range(planes):
            slope_ref[plane] = silu_slope(pre[plane])
        pairs = (
            lax.broadcasted_iota(jnp.int32, (depth, low_depth), 0) // 2
            == lax.broadcasted_iota(jnp.int32, (depth, low_depth), 1)
        ).astype(BF16)
        for plane in range(low_planes):
            for row in range(low_y):
                rows = jnp.concatenate(
                    [
                        hidden[2 * plane + x][:, (2 * row + y) * depth : (2 * row + y + 1) * depth]
                        for x in range(2)
                        for y in range(2)
                    ],
                    axis=0,
                )
                sums = dot(rows, pairs)
                total = sums[:channels]
                for piece in range(1, 4):
                    total = total + sums[piece * channels : (piece + 1) * channels]
                pooled_ref[:, row * low_depth : (row + 1) * low_depth] = (0.125 * total).astype(
                    BF16
                )

    pooled, slope, whole = call(
        first_kernel,
        (
            shaped((channels, low_cells), BF16),
            shaped((planes, channels, fine_cells), F32),
            shaped((planes + 2, channels, fine_cells), BF16),
        ),
        name="first_conv",
    )(*own, *halo_a, *halo_b, first_forward)

    pool_a, pool_b = swap_a(pooled), swap_b(pooled)

    def second_kernel(own_ref, a_ref, b_ref, matrices, cot_ref, out_ref, down_ref):
        left, right = ordered_halos(a_ref[...], b_ref[...])
        stacks = [stack3(value, low_depth) for value in (left, own_ref[...], right)]
        (pre,) = conv_planes(matrices, stacks, 1, filters, low_depth)
        out_ref[...] = silu(pre).astype(BF16)
        down_ref[...] = (cot_ref[...].astype(F32) * silu_slope(pre)).astype(BF16)

    features, down = call(
        second_kernel,
        (shaped((filters, low_cells), BF16), shaped((filters, low_cells), BF16)),
        name="second_conv",
    )(pooled, pool_a, pool_b, second_forward, low_cot)
    features = features.reshape(filters, 1, low_y, low_depth)

    down_a, down_b = swap_a(down), swap_b(down)

    first_rows, second_rows = 9 * channels, 9 * filters
    packed_first, packed_second = first_rows * 3 // 2, second_rows * 3 // 2
    second_side = space // 4
    unit = 16 * space
    total_rows = -(-(packed_first + packed_second) // unit) * unit
    quarter = total_rows // 4
    chunk = total_rows // space

    def second_weight_kernel(down_ref, own_ref, a_ref, b_ref, out_ref, acc):
        left, right = ordered_halos(a_ref[...], b_ref[...])
        stacks = [stack3(value, low_depth) for value in (left, own_ref[...], right)]
        weight_planes(acc, [down_ref[...]], stacks, low_depth)
        pack(acc, out_ref, 0, second_rows)

    second_part = call(
        second_weight_kernel,
        shaped((packed_second, 128), F32),
        (pltpu.VMEM((second_rows, 3 * channels), F32),),
        name="second_weight",
    )(down, pooled, pool_a, pool_b)

    def group_kernel(own_ref, a_ref, b_ref, matrices, out_ref):
        left, right = ordered_halos(a_ref[...], b_ref[...])
        stacks = [stack3(value, low_depth) for value in (left, own_ref[...], right)]
        (part,) = conv_planes(matrices, stacks, 1, channels, low_depth)
        out_ref[...] = part.astype(BF16)

    part = call(group_kernel, shaped((channels, low_cells), BF16), name="group_part")(
        down, down_a, down_b, second_back
    )
    parts = [part] + [
        lax.ppermute(part, "filt", [(f, f ^ slot) for f in range(filt)])
        for slot in range(1, filt)
    ]

    def grad_kernel(*refs):
        part_refs = refs[:filt]
        slope_ref, whole_ref, second_ref = refs[filt : filt + 3]
        down_ref, edge_a_ref, edge_b_ref = refs[filt + 3 : filt + 6]
        own_ref = refs[filt + 6]
        send_refs = refs[filt + 7 : filt + 10]
        acc, rows_ref = refs[filt + 10 :]
        spread = (
            lax.broadcasted_iota(jnp.int32, (low_depth, depth), 0)
            == lax.broadcasted_iota(jnp.int32, (low_depth, depth), 1) // 2
        ).astype(BF16)
        columns = []
        for row in range(low_y):
            wide = None
            for ref in part_refs:
                term = dot(ref[:, row * low_depth : (row + 1) * low_depth], spread)
                wide = term if wide is None else wide + term
            columns += [0.125 * wide] * 2
        hidden_grad = jnp.concatenate(columns, axis=1)
        grads = [(hidden_grad * slope_ref[p]).astype(BF16) for p in range(planes)]
        for plane in range(planes):
            down_ref[plane] = grads[plane]
        odd = lax.axis_index("space") % 2
        edge_a_ref[...] = jnp.where(odd == 1, grads[0], grads[planes - 1])
        edge_b_ref[...] = jnp.where(odd == 1, grads[planes - 1], grads[0])
        stacks = [stack3(whole_ref[p], depth) for p in range(planes + 2)]
        weight_planes(acc, grads, stacks, depth)
        pack(acc, rows_ref, 0, first_rows)
        rows_ref[packed_first : packed_first + packed_second, :] = second_ref[...]
        if total_rows > packed_first + packed_second:
            rows_ref[packed_first + packed_second :, :] = jnp.zeros(
                (total_rows - packed_first - packed_second, 128), F32
            )
        low = lax.axis_index("space") % 4
        own_ref[...] = rows_ref[pl.ds(pl.multiple_of(low * quarter, 16), quarter), :]
        for k in range(1, 4):
            start = pl.multiple_of((low ^ k) * quarter, 16)
            send_refs[k - 1][...] = rows_ref[pl.ds(start, quarter), :].astype(BF16)

    first_down, fine_edge_a, fine_edge_b, own_rows, *sends = call(
        grad_kernel,
        (
            shaped((planes, channels, fine_cells), BF16),
            shaped((channels, fine_cells), BF16),
            shaped((channels, fine_cells), BF16),
            shaped((quarter, 128), F32),
        )
        + (shaped((quarter, 128), BF16),) * 3,
        (
            pltpu.VMEM((first_rows, 3 * channels), F32),
            pltpu.VMEM((total_rows, 128), F32),
        ),
        name="first_weight",
    )(*parts, slope, whole, second_part)

    near = [[(i, i ^ k) for i in range(space)] for k in range(4)]
    far = [[(i, i ^ (4 * k)) for i in range(space)] for k in range(second_side)]
    got = [lax.ppermute(sends[k - 1], "space", near[k]) for k in range(1, 4)]
    down_halo_a, down_halo_b = swap_a(fine_edge_a), swap_b(fine_edge_b)

    def fold_kernel(own_ref, *refs):
        got_refs, out_refs, rows_ref = refs[:3], refs[3:-1], refs[-1]
        total = own_ref[...]
        for ref in got_refs:
            total = total + ref[...].astype(F32)
        rows_ref[...] = total
        high = lax.axis_index("space") // 4
        out_refs[0][...] = rows_ref[pl.ds(pl.multiple_of(high * chunk, 16), chunk), :]
        for k in range(1, second_side):
            start = pl.multiple_of((high ^ k) * chunk, 16)
            out_refs[k][...] = rows_ref[pl.ds(start, chunk), :].astype(BF16)

    own_chunk, *sends = call(
        fold_kernel,
        (shaped((chunk, 128), F32),) + (shaped((chunk, 128), BF16),) * (second_side - 1),
        (pltpu.VMEM((quarter, 128), F32),),
        name="fold_near",
    )(own_rows, *got)
    got = [lax.ppermute(sends[k - 1], "space", far[k]) for k in range(1, second_side)]

    def volume_kernel(own_ref, a_ref, b_ref, matrices, out_ref, rows_ref):
        left, right = ordered_halos(a_ref[...], b_ref[...])
        values = [left] + [own_ref[p] for p in range(planes)] + [right]
        blank = jnp.zeros((channels, depth), BF16)
        begin = pl.multiple_of(lax.axis_index("filt") * brick, brick)
        stacks = []
        for position, value in enumerate(values):
            rows_ref[position] = jnp.concatenate([blank, value, blank], axis=1)
            stacks.append(stack3(rows_ref[position, :, pl.ds(begin, brick + 2 * depth)], depth))
        results = conv_planes(matrices, stacks, planes, channels, depth)
        for plane in range(planes):
            out_ref[plane] = results[plane][:, depth : depth + brick].astype(BF16)

    volume_grad = call(
        volume_kernel,
        shaped((planes, channels, brick), BF16),
        (halves((planes + 2, channels, fine_cells + 2 * depth)),),
        name="volume_grad",
    )(first_down, down_halo_a, down_halo_b, first_back)
    volume_grad = jnp.transpose(
        volume_grad.reshape(planes, channels, brick_y, depth), (1, 0, 2, 3)
    )

    def sum_kernel(own_ref, *refs):
        total = own_ref[...]
        for ref in refs[:-1]:
            total = total + ref[...].astype(F32)
        refs[-1][...] = total.astype(BF16)

    final_chunk = call(sum_kernel, shaped((chunk, 128), BF16), name="fold_far")(own_chunk, *got)
    pieces = [final_chunk] + [
        lax.ppermute(final_chunk, "space", far[k]) for k in range(1, second_side)
    ]

    def join_kernel(*refs):
        high = lax.axis_index("space") // 4
        for k, ref in enumerate(refs[:-1]):
            refs[-1][pl.ds(pl.multiple_of((high ^ k) * chunk, 16), chunk), :] = ref[...]

    group = call(join_kernel, shaped((quarter, 128), BF16), name="join_far")(*pieces)
    pieces = [group] + [lax.ppermute(group, "space", near[k]) for k in range(1, 4)]

    def final_kernel(*refs):
        first_ref, second_ref, rows_ref = refs[4:]
        low = lax.axis_index("space") % 4
        for k, ref in enumerate(refs[:4]):
            rows_ref[pl.ds(pl.multiple_of((low ^ k) * quarter, 16), quarter), :] = ref[...].astype(
                F32
            )
        unpack(rows_ref, 0, first_rows, first_ref, fine_scale)
        unpack(rows_ref, packed_first, second_rows, second_ref, low_scale)

    first_grad, second_grad = call(
        final_kernel,
        (shaped((27, channels, channels), F32), shaped((27, filters, channels), F32)),
        (pltpu.VMEM((total_rows, 128), F32),),
        name="join_near",
    )(*pieces)
    return (features, volume_grad, first_grad, second_grad)


def solution(mesh):
    placed = (
        P(None, "space", "filt", None),
        P(),
        P(None, "filt", None),
        P("filt", "space", None, None),
    )
    return jax.shard_map(
        functools.partial(local, mesh.shape["space"], mesh.shape["filt"]),
        mesh=mesh,
        in_specs=placed,
        out_specs=(
            P("filt", "space", None, None),
            P(None, "space", "filt", None),
            P(),
            P(None, "filt", None),
        ),
        check_vma=False,
    )
```

```python
import functools

import jax
import jax.numpy as jnp
from jax import lax
from jax.experimental import pallas as pl
from jax.experimental.pallas import tpu as pltpu
from jax.sharding import PartitionSpec as P

F32 = jnp.float32
BF16 = jnp.bfloat16
VMEM_LIMIT = 56 * 1024 * 1024


def call(body, outs, scratch=(), name=None):
    def run(*args):
        kernel = pl.pallas_call(
            body,
            out_shape=outs,
            in_specs=[pl.BlockSpec(memory_space=pltpu.VMEM)] * len(args),
            out_specs=jax.tree.map(lambda _: pl.BlockSpec(memory_space=pltpu.VMEM), outs),
            scratch_shapes=scratch,
            name=name,
            compiler_params=pltpu.CompilerParams(vmem_limit_bytes=VMEM_LIMIT),
        )
        return kernel(*[pltpu.with_memory_space_constraint(arg, pltpu.VMEM) for arg in args])

    return run


def shaped(shape, dtype):
    return pltpu.VMEM(shape, dtype)


def dot(lhs, rhs):
    return jnp.dot(lhs, rhs, preferred_element_type=F32)


def dot_cells(lhs, rhs):
    return lax.dot_general(lhs, rhs, (((1,), (1,)), ((), ())), preferred_element_type=F32)


def silu_slope(values):
    part = 1.0 / (1.0 + jnp.exp(-values))
    return part * (1.0 + values * (1.0 - part))


def silu(values):
    return values / (1.0 + jnp.exp(-values))


def stack3(cells, depth):
    count = cells.shape[1]
    lane = lax.broadcasted_iota(jnp.int32, cells.shape, 1) % depth
    wide = cells.astype(F32)
    below = jnp.where(lane == 0, 0.0, pltpu.roll(wide, 1, 1)).astype(BF16)
    above = jnp.where(lane == depth - 1, 0.0, pltpu.roll(wide, count - 1, 1)).astype(BF16)
    return jnp.concatenate([below, cells, above], axis=0)


def shifted_rows(cells, offset, depth):
    if offset == 0:
        return cells
    blank = jnp.zeros((cells.shape[0], depth), cells.dtype)
    if cells.shape[1] == depth:
        return blank
    if offset > 0:
        return jnp.concatenate([cells[:, depth:], blank], axis=1)
    return jnp.concatenate([blank, cells[:, :-depth]], axis=1)


def conv_planes(matrices, stacks, planes, outputs, depth):
    results = [None] * planes
    for place in range(planes + 2):
        first = max(0, place - planes + 1)
        last = min(2, place)
        rows = matrices[first * 3 * outputs : (last + 1) * 3 * outputs, :]
        terms = dot(rows, stacks[place])
        for tap_x in range(first, last + 1):
            for tap_y in range(3):
                begin = ((tap_x - first) * 3 + tap_y) * outputs
                term = shifted_rows(terms[begin : begin + outputs], tap_y - 1, depth)
                target = place - tap_x
                results[target] = term if results[target] is None else results[target] + term
    return results


def weight_planes(acc, grads, stacks, depth):
    planes = len(grads)
    outputs = grads[0].shape[0]
    rows = [
        jnp.concatenate([shifted_rows(grad, 1 - tap_y, depth) for tap_y in range(3)], axis=0)
        for grad in grads
    ]
    for tap_x in range(3):
        total = None
        for plane in range(planes):
            term = dot_cells(rows[plane], stacks[plane + tap_x])
            total = term if total is None else total + term
        acc[tap_x * 3 * outputs : (tap_x + 1) * 3 * outputs, :] = total


def pack(acc, target, base, rows):
    half = rows // 2
    target[base : base + rows, :] = acc[:, :128]
    target[base + rows : base + rows + half, :] = jnp.concatenate(
        [acc[:half, 128:], acc[half:, 128:]], axis=1
    )


def unpack(source, base, rows, out, scale):
    half = rows // 2
    outputs = rows // 9
    for pair in range(9):
        main = source[base + pair * outputs : base + (pair + 1) * outputs, :].astype(F32) * scale
        out[3 * pair] = main[:, :64]
        out[3 * pair + 1] = main[:, 64:]
    for piece in range(0, 9 * outputs, 8):
        row = piece if piece < half else piece - half
        tail = source[base + rows + row : base + rows + row + 8, :].astype(F32) * scale
        side = tail[:, :64] if piece < half else tail[:, 64:]
        out[3 * (piece // outputs) + 2, piece % outputs : piece % outputs + 8, :] = side


def halo_places():
    index = lax.axis_index("space")
    ends = lax.axis_size("space") - 1
    a_right = 1 - index % 2
    inside = jnp.logical_and(index > 0, index < ends)
    return a_right, inside


def ordered_halos(got_a, got_b):
    a_right, inside = halo_places()
    got_b = jnp.where(inside, got_b, jnp.zeros_like(got_b))
    left = jnp.where(a_right == 1, got_b, got_a)
    right = jnp.where(a_right == 1, got_a, got_b)
    return left, right


def swap_tables(count):
    table_a = [(i, i ^ 1) for i in range(count)]
    table_b = [(0, 0)]
    for i in range(1, count - 1, 2):
        table_b += [(i, i + 1), (i + 1, i)]
    table_b.append((count - 1, count - 1))
    return table_a, table_b


def halves(shape):
    return pltpu.VMEM(shape, BF16)


def join_rows(target, place, pieces, brick):
    index = lax.axis_index("filt")
    for slot, piece in enumerate(pieces):
        start = pl.multiple_of((index ^ slot) * brick, brick)
        target[place, :, pl.ds(start, brick)] = piece


def local(space, filt, volume, first_weight, second_weight, cotangent):
    channels, planes, brick_y, depth = volume.shape
    filters = second_weight.shape[1]
    table_a, table_b = swap_tables(space)
    fine_y = brick_y * filt
    low_y = fine_y // 2
    low_depth = depth // 2
    fine_cells = fine_y * depth
    low_cells = low_y * low_depth
    brick = brick_y * depth
    fine_scale = 1.0 / (planes * space * fine_cells) ** 0.5
    low_scale = 1.0 / (planes // 2 * space * low_cells) ** 0.5
    low_planes = planes // 2

    def swap_a(piece):
        return lax.ppermute(piece, "space", table_a)

    def swap_b(piece):
        return lax.ppermute(piece, "space", table_b)

    def both(table, slot):
        return [(i * filt + f, j * filt + (f ^ slot)) for i, j in table for f in range(filt)]

    def across(piece, table, slot):
        return lax.ppermute(piece, ("space", "filt"), both(table, slot))

    place = lax.axis_index("space")
    own_table = [(i, i) for i in range(space)]
    brick_rows = jnp.transpose(volume, (1, 0, 2, 3)).reshape(planes, channels, brick)
    odd = place % 2
    edge_a = jnp.where(odd == 1, brick_rows[0], brick_rows[planes - 1])
    edge_b = jnp.where(odd == 1, brick_rows[planes - 1], brick_rows[0])
    own = [brick_rows] + [across(brick_rows, own_table, slot) for slot in range(1, filt)]
    halo_a = [across(edge_a, table_a, slot) for slot in range(filt)]
    halo_b = [across(edge_b, table_b, slot) for slot in range(filt)]

    first_taps = first_weight.reshape(9, 3, channels, channels)
    first_forward = jnp.transpose(first_taps, (0, 2, 1, 3)).reshape(9 * channels, 3 * channels)
    first_back = jnp.transpose(first_taps[::-1, ::-1], (0, 3, 1, 2)).reshape(
        9 * channels, 3 * channels
    )
    second_taps = second_weight.reshape(9, 3, filters, channels)
    second_forward = jnp.transpose(second_taps, (0, 2, 1, 3)).reshape(9 * filters, 3 * channels)
    second_back = jnp.transpose(second_taps[::-1, ::-1], (0, 3, 1, 2)).reshape(
        9 * channels, 3 * filters
    )
    low_cot = cotangent.reshape(filters, low_cells)

    def first_kernel(*refs):
        own_refs = refs[:filt]
        a_refs = refs[filt : 2 * filt]
        b_refs = refs[2 * filt : 3 * filt]
        matrices, pooled_ref, slope_ref, whole_ref = refs[3 * filt : 3 * filt + 4]
        for plane in range(planes):
            join_rows(whole_ref, 1 + plane, [ref[plane] for ref in own_refs], brick)
        halos = [ordered_halos(a[...], b[...]) for a, b in zip(a_refs, b_refs)]
        join_rows(whole_ref, 0, [pair[0] for pair in halos], brick)
        join_rows(whole_ref, planes + 1, [pair[1] for pair in halos], brick)
        stacks = [stack3(whole_ref[p], depth) for p in range(planes + 2)]
        pre = conv_planes(matrices, stacks, planes, channels, depth)
        hidden = [silu(value).astype(BF16) for value in pre]
        for plane in range(planes):
            slope_ref[plane] = silu_slope(pre[plane])
        pairs = (
            lax.broadcasted_iota(jnp.int32, (depth, low_depth), 0) // 2
            == lax.broadcasted_iota(jnp.int32, (depth, low_depth), 1)
        ).astype(BF16)
        for plane in range(low_planes):
            for row in range(low_y):
                rows = jnp.concatenate(
                    [
                        hidden[2 * plane + x][:, (2 * row + y) * depth : (2 * row + y + 1) * depth]
                        for x in range(2)
                        for y in range(2)
                    ],
                    axis=0,
                )
                sums = dot(rows, pairs)
                total = sums[:channels]
                for piece in range(1, 4):
                    total = total + sums[piece * channels : (piece + 1) * channels]
                pooled_ref[:, row * low_depth : (row + 1) * low_depth] = (0.125 * total).astype(
                    BF16
                )

    pooled, slope, whole = call(
        first_kernel,
        (
            shaped((channels, low_cells), BF16),
            shaped((planes, channels, fine_cells), F32),
            shaped((planes + 2, channels, fine_cells), BF16),
        ),
        name="first_conv",
    )(*own, *halo_a, *halo_b, first_forward)

    pool_a, pool_b = swap_a(pooled), swap_b(pooled)

    def second_kernel(own_ref, a_ref, b_ref, matrices, cot_ref, out_ref, down_ref):
        left, right = ordered_halos(a_ref[...], b_ref[...])
        stacks = [stack3(value, low_depth) for value in (left, own_ref[...], right)]
        (pre,) = conv_planes(matrices, stacks, 1, filters, low_depth)
        out_ref[...] = silu(pre).astype(BF16)
        down_ref[...] = (cot_ref[...].astype(F32) * silu_slope(pre)).astype(BF16)

    features, down = call(
        second_kernel,
        (shaped((filters, low_cells), BF16), shaped((filters, low_cells), BF16)),
        name="second_conv",
    )(pooled, pool_a, pool_b, second_forward, low_cot)
    features = features.reshape(filters, 1, low_y, low_depth)

    down_a, down_b = swap_a(down), swap_b(down)

    first_rows, second_rows = 9 * channels, 9 * filters
    packed_first, packed_second = first_rows * 3 // 2, second_rows * 3 // 2
    second_side = space // 4
    unit = 16 * space
    total_rows = -(-(packed_first + packed_second) // unit) * unit
    quarter = total_rows // 4
    chunk = total_rows // space

    def second_weight_kernel(down_ref, own_ref, a_ref, b_ref, out_ref, acc):
        left, right = ordered_halos(a_ref[...], b_ref[...])
        stacks = [stack3(value, low_depth) for value in (left, own_ref[...], right)]
        weight_planes(acc, [down_ref[...]], stacks, low_depth)
        pack(acc, out_ref, 0, second_rows)

    second_part = call(
        second_weight_kernel,
        shaped((packed_second, 128), F32),
        (pltpu.VMEM((second_rows, 3 * channels), F32),),
        name="second_weight",
    )(down, pooled, pool_a, pool_b)

    def group_kernel(own_ref, a_ref, b_ref, matrices, out_ref):
        left, right = ordered_halos(a_ref[...], b_ref[...])
        stacks = [stack3(value, low_depth) for value in (left, own_ref[...], right)]
        (part,) = conv_planes(matrices, stacks, 1, channels, low_depth)
        out_ref[...] = part.astype(BF16)

    part = call(group_kernel, shaped((channels, low_cells), BF16), name="group_part")(
        down, down_a, down_b, second_back
    )
    parts = [part] + [
        lax.ppermute(part, "filt", [(f, f ^ slot) for f in range(filt)])
        for slot in range(1, filt)
    ]

    def grad_kernel(*refs):
        part_refs = refs[:filt]
        slope_ref, whole_ref, second_ref = refs[filt : filt + 3]
        down_ref, edge_a_ref, edge_b_ref = refs[filt + 3 : filt + 6]
        own_ref = refs[filt + 6]
        send_refs = refs[filt + 7 : filt + 10]
        acc, rows_ref = refs[filt + 10 :]
        spread = (
            lax.broadcasted_iota(jnp.int32, (low_depth, depth), 0)
            == lax.broadcasted_iota(jnp.int32, (low_depth, depth), 1) // 2
        ).astype(BF16)
        columns = []
        for row in range(low_y):
            wide = None
            for ref in part_refs:
                term = dot(ref[:, row * low_depth : (row + 1) * low_depth], spread)
                wide = term if wide is None else wide + term
            columns += [0.125 * wide] * 2
        hidden_grad = jnp.concatenate(columns, axis=1)
        grads = [(hidden_grad * slope_ref[p]).astype(BF16) for p in range(planes)]
        for plane in range(planes):
            down_ref[plane] = grads[plane]
        odd = lax.axis_index("space") % 2
        edge_a_ref[...] = jnp.where(odd == 1, grads[0], grads[planes - 1])
        edge_b_ref[...] = jnp.where(odd == 1, grads[planes - 1], grads[0])
        stacks = [stack3(whole_ref[p], depth) for p in range(planes + 2)]
        weight_planes(acc, grads, stacks, depth)
        pack(acc, rows_ref, 0, first_rows)
        rows_ref[packed_first : packed_first + packed_second, :] = second_ref[...]
        if total_rows > packed_first + packed_second:
            rows_ref[packed_first + packed_second :, :] = jnp.zeros(
                (total_rows - packed_first - packed_second, 128), F32
            )
        low = lax.axis_index("space") % 4
        own_ref[...] = rows_ref[pl.ds(pl.multiple_of(low * quarter, 16), quarter), :]
        for k in range(1, 4):
            start = pl.multiple_of((low ^ k) * quarter, 16)
            send_refs[k - 1][...] = rows_ref[pl.ds(start, quarter), :].astype(BF16)

    first_down, fine_edge_a, fine_edge_b, own_rows, *sends = call(
        grad_kernel,
        (
            shaped((planes, channels, fine_cells), BF16),
            shaped((channels, fine_cells), BF16),
            shaped((channels, fine_cells), BF16),
            shaped((quarter, 128), F32),
        )
        + (shaped((quarter, 128), BF16),) * 3,
        (
            pltpu.VMEM((first_rows, 3 * channels), F32),
            pltpu.VMEM((total_rows, 128), F32),
        ),
        name="first_weight",
    )(*parts, slope, whole, second_part)

    near = [[(i, i ^ k) for i in range(space)] for k in range(4)]
    far = [[(i, i ^ (4 * k)) for i in range(space)] for k in range(second_side)]
    got = [lax.ppermute(sends[k - 1], "space", near[k]) for k in range(1, 4)]
    down_halo_a, down_halo_b = swap_a(fine_edge_a), swap_b(fine_edge_b)

    def fold_kernel(own_ref, *refs):
        got_refs, out_refs, rows_ref = refs[:3], refs[3:-1], refs[-1]
        total = own_ref[...]
        for ref in got_refs:
            total = total + ref[...].astype(F32)
        rows_ref[...] = total
        high = lax.axis_index("space") // 4
        out_refs[0][...] = rows_ref[pl.ds(pl.multiple_of(high * chunk, 16), chunk), :]
        for k in range(1, second_side):
            start = pl.multiple_of((high ^ k) * chunk, 16)
            out_refs[k][...] = rows_ref[pl.ds(start, chunk), :].astype(BF16)

    own_chunk, *sends = call(
        fold_kernel,
        (shaped((chunk, 128), F32),) + (shaped((chunk, 128), BF16),) * (second_side - 1),
        (pltpu.VMEM((quarter, 128), F32),),
        name="fold_near",
    )(own_rows, *got)
    got = [lax.ppermute(sends[k - 1], "space", far[k]) for k in range(1, second_side)]

    def volume_kernel(own_ref, a_ref, b_ref, matrices, out_ref, rows_ref):
        left, right = ordered_halos(a_ref[...], b_ref[...])
        values = [left] + [own_ref[p] for p in range(planes)] + [right]
        blank = jnp.zeros((channels, depth), BF16)
        begin = pl.multiple_of(lax.axis_index("filt") * brick, brick)
        stacks = []
        for position, value in enumerate(values):
            rows_ref[position] = jnp.concatenate([blank, value, blank], axis=1)
            stacks.append(stack3(rows_ref[position, :, pl.ds(begin, brick + 2 * depth)], depth))
        results = conv_planes(matrices, stacks, planes, channels, depth)
        for plane in range(planes):
            out_ref[plane] = results[plane][:, depth : depth + brick].astype(BF16)

    volume_grad = call(
        volume_kernel,
        shaped((planes, channels, brick), BF16),
        (halves((planes + 2, channels, fine_cells + 2 * depth)),),
        name="volume_grad",
    )(first_down, down_halo_a, down_halo_b, first_back)
    volume_grad = jnp.transpose(
        volume_grad.reshape(planes, channels, brick_y, depth), (1, 0, 2, 3)
    )

    def sum_kernel(own_ref, *refs):
        total = own_ref[...]
        for ref in refs[:-1]:
            total = total + ref[...].astype(F32)
        refs[-1][...] = total.astype(BF16)

    final_chunk = call(sum_kernel, shaped((chunk, 128), BF16), name="fold_far")(own_chunk, *got)
    pieces = [final_chunk] + [
        lax.ppermute(final_chunk, "space", far[k]) for k in range(1, second_side)
    ]

    def join_kernel(*refs):
        high = lax.axis_index("space") // 4
        for k, ref in enumerate(refs[:-1]):
            refs[-1][pl.ds(pl.multiple_of((high ^ k) * chunk, 16), chunk), :] = ref[...]

    group = call(join_kernel, shaped((quarter, 128), BF16), name="join_far")(*pieces)
    pieces = [group] + [lax.ppermute(group, "space", near[k]) for k in range(1, 4)]

    def final_kernel(*refs):
        first_ref, second_ref, rows_ref = refs[4:]
        low = lax.axis_index("space") % 4
        for k, ref in enumerate(refs[:4]):
            rows_ref[pl.ds(pl.multiple_of((low ^ k) * quarter, 16), quarter), :] = ref[...].astype(
                F32
            )
        unpack(rows_ref, 0, first_rows, first_ref, fine_scale)
        unpack(rows_ref, packed_first, second_rows, second_ref, low_scale)

    first_grad, second_grad = call(
        final_kernel,
        (shaped((27, channels, channels), F32), shaped((27, filters, channels), F32)),
        (pltpu.VMEM((total_rows, 128), F32),),
        name="join_near",
    )(*pieces)
    return (features, volume_grad, first_grad, second_grad)


def solution(mesh):
    placed = (
        P(None, "space", "filt", None),
        P(),
        P(None, "filt", None),
        P("filt", "space", None, None),
    )
    return jax.shard_map(
        functools.partial(local, mesh.shape["space"], mesh.shape["filt"]),
        mesh=mesh,
        in_specs=placed,
        out_specs=(
            P("filt", "space", None, None),
            P(None, "space", "filt", None),
            P(),
            P(None, "filt", None),
        ),
        check_vma=False,
    )
```

```python
import jax
import jax.numpy as jnp
from jax import lax
from jax.experimental import pallas as pl
from jax.experimental.pallas import tpu as pltpu
from jax.sharding import PartitionSpec as P


F32 = jnp.float32
BF16 = jnp.bfloat16
VMEM_LIMIT = 32 * 1024 * 1024


def call(body, outs, scratch=()):
    def run(*args):
        return pl.pallas_call(
            body,
            out_shape=outs,
            in_specs=[pl.BlockSpec(memory_space=pltpu.VMEM)] * len(args),
            scratch_shapes=scratch,
            compiler_params=pltpu.CompilerParams(vmem_limit_bytes=VMEM_LIMIT),
        )(*[pltpu.with_memory_space_constraint(arg, pltpu.VMEM) for arg in args])

    return run


def shaped(shape, dtype):
    return pltpu.VMEM(shape, dtype)


def dot(lhs, rhs):
    return jnp.dot(lhs, rhs, preferred_element_type=F32)


def dot_cells(lhs, rhs):
    return lax.dot_general(lhs, rhs, (((1,), (1,)), ((), ())), preferred_element_type=F32)


def silu_slope(values):
    part = 1.0 / (1.0 + jnp.exp(-values))
    return part * (1.0 + values * (1.0 - part))


def silu(values):
    return values / (1.0 + jnp.exp(-values))


def stack3(cells, depth):
    count = cells.shape[1]
    lane = lax.broadcasted_iota(jnp.int32, cells.shape, 1) % depth
    wide = cells.astype(F32)
    below = jnp.where(lane == 0, 0.0, pltpu.roll(wide, 1, 1)).astype(BF16)
    above = jnp.where(lane == depth - 1, 0.0, pltpu.roll(wide, count - 1, 1)).astype(BF16)
    return jnp.concatenate([below, cells, above], axis=0)


def shifted_rows(cells, offset, depth):
    if offset == 0:
        return cells
    blank = jnp.zeros((cells.shape[0], depth), cells.dtype)
    if cells.shape[1] == depth:
        return blank
    if offset > 0:
        return jnp.concatenate([cells[:, depth:], blank], axis=1)
    return jnp.concatenate([blank, cells[:, :-depth]], axis=1)


def conv_planes(matrices, stacks, planes, outputs, depth):
    results = [None] * planes
    for place in range(planes + 2):
        first = max(0, place - planes + 1)
        last = min(2, place)
        rows = matrices[first * 3 * outputs : (last + 1) * 3 * outputs, :]
        terms = dot(rows, stacks[place])
        for tap_x in range(first, last + 1):
            for tap_y in range(3):
                begin = ((tap_x - first) * 3 + tap_y) * outputs
                term = shifted_rows(terms[begin : begin + outputs], tap_y - 1, depth)
                target = place - tap_x
                results[target] = term if results[target] is None else results[target] + term
    return results


def weight_planes(acc, grads, stacks, depth):
    planes = len(grads)
    outputs = grads[0].shape[0]
    rows = [
        jnp.concatenate([shifted_rows(grad, 1 - tap_y, depth) for tap_y in range(3)], axis=0)
        for grad in grads
    ]
    for tap_x in range(3):
        total = None
        for plane in range(planes):
            term = dot_cells(rows[plane], stacks[plane + tap_x])
            total = term if total is None else total + term
        acc[tap_x * 3 * outputs : (tap_x + 1) * 3 * outputs, :] = total


def pack(acc, target, base, rows):
    half = rows // 2
    target[base : base + rows, :] = acc[:, :128]
    target[base + rows : base + rows + half, :] = jnp.concatenate(
        [acc[:half, 128:], acc[half:, 128:]], axis=1
    )


def unpack(source, base, rows, out, scale):
    half = rows // 2
    outputs = rows // 9
    for pair in range(9):
        main = source[base + pair * outputs : base + (pair + 1) * outputs, :].astype(F32) * scale
        out[3 * pair] = main[:, :64]
        out[3 * pair + 1] = main[:, 64:]
    for piece in range(0, 9 * outputs, 8):
        row = piece if piece < half else piece - half
        tail = source[base + rows + row : base + rows + row + 8, :].astype(F32) * scale
        side = tail[:, :64] if piece < half else tail[:, 64:]
        out[3 * (piece // outputs) + 2, piece % outputs : piece % outputs + 8, :] = side


def forward_matrix(taps, target, outputs):
    for pair in range(9):
        target[pair * outputs : (pair + 1) * outputs, :] = jnp.concatenate(
            [taps[3 * pair + tap_z] for tap_z in range(3)], axis=1
        )


def backward_matrix(taps):
    rows = [
        jnp.concatenate([taps[26 - 3 * pair - tap_z] for pair in range(9)], axis=1)
        for tap_z in range(3)
    ]
    return jnp.concatenate(rows, axis=0).T


def pick(flag, one, other):
    return jnp.where(flag, one, other)


def swap_tables(count):
    ends = [(0, 0), (count - 1, count - 1)]
    table_b = ends + [(i, i + 1) for i in range(1, count - 1, 2)]
    table_b += [(i + 1, i) for i in range(1, count - 1, 2)]
    low = [i for i in range(count - 2) if i % 4 >= 2]
    table_d = [(i, i + 2) for i in low] + [(i + 2, i) for i in low]
    table_d += [(0, 0), (1, 1), (count - 2, count - 2), (count - 1, count - 1)]
    return table_b, table_d


def join_rows(target, place, pieces, brick):
    index = lax.axis_index("filt")
    for slot, piece in enumerate(pieces):
        start = pl.multiple_of((index ^ slot) * brick, brick)
        target[place, :, pl.ds(start, brick)] = piece


def local(space, filt, volume, first_weight, second_weight, cotangent):
    channels, planes, brick_y, depth = volume.shape
    filters = second_weight.shape[1]
    fine_y = brick_y * filt
    low_y = fine_y // 2
    low_depth = depth // 2
    fine_cells = fine_y * depth
    low_cells = low_y * low_depth
    brick = brick_y * depth
    fine_scale = 1.0 / (planes * space * fine_cells) ** 0.5
    low_scale = 1.0 / (planes // 2 * space * low_cells) ** 0.5
    blocks = channels // filters
    extra = low_cells // blocks
    table_b, table_d = swap_tables(space)

    def mirror(mask):
        return [(i, i ^ mask) for i in range(space)]

    def along(piece, table):
        return lax.ppermute(piece, "space", table)

    def across(piece, table, slot):
        pairs = [(i * filt + f, j * filt + (f ^ slot)) for i, j in table for f in range(filt)]
        return lax.ppermute(piece, ("space", "filt"), pairs)

    place = lax.axis_index("space")
    bricks = jnp.transpose(volume, (1, 0, 2, 3)).reshape(planes, channels, brick)
    cot = cotangent.reshape(filters, blocks, extra)
    cot = jnp.transpose(cot, (1, 0, 2)).reshape(channels, extra)
    edge = jnp.where(place % 2 == 1, bricks[planes - 1], bricks[0])
    own_message = jnp.concatenate([bricks[p] for p in range(planes)] + [cot], axis=1)
    edge_message = jnp.concatenate([edge, cot], axis=1)
    own = [own_message] + [across(own_message, mirror(0), slot) for slot in range(1, filt)]
    side_b = [across(edge_message, table_b, slot) for slot in range(filt)]
    side_a = [along(message, mirror(1)) for message in own]

    narrow = jnp.concatenate([second_weight[:14], second_weight[13:]], axis=2)
    narrows = [narrow] + [across(narrow, mirror(0), slot) for slot in range(1, filt)]

    def first_kernel(*refs):
        own_refs, a_refs, b_refs = refs[:filt], refs[filt : 2 * filt], refs[2 * filt : 3 * filt]
        taps, pooled_ref, slope_ref, whole_ref, matrices = refs[3 * filt :]
        index = lax.axis_index("space")
        odd = index % 2 == 1
        inside = jnp.logical_and(index > 0, index < space - 1)
        forward_matrix(taps, matrices, channels)
        for plane in range(planes):
            pieces = [ref[:, plane * brick : (plane + 1) * brick] for ref in own_refs]
            join_rows(whole_ref, 1 + plane, pieces, brick)
        lefts, rights = [], []
        for a_ref, b_ref in zip(a_refs, b_refs):
            got_a = pick(odd, a_ref[:, (planes - 1) * brick : planes * brick], a_ref[:, :brick])
            got_b = b_ref[:, :brick]
            got_b = pick(inside, got_b, jnp.zeros_like(got_b))
            lefts.append(pick(odd, got_a, got_b))
            rights.append(pick(odd, got_b, got_a))
        join_rows(whole_ref, 0, lefts, brick)
        join_rows(whole_ref, planes + 1, rights, brick)
        stacks = [stack3(whole_ref[p], depth) for p in range(planes + 2)]
        pre = conv_planes(matrices, stacks, planes, channels, depth)
        hidden = [silu(value).astype(BF16) for value in pre]
        for plane in range(planes):
            slope_ref[plane] = silu_slope(pre[plane])
        pairs = (
            lax.broadcasted_iota(jnp.int32, (depth, low_depth), 0) // 2
            == lax.broadcasted_iota(jnp.int32, (depth, low_depth), 1)
        ).astype(BF16)
        for row in range(low_y):
            rows = jnp.concatenate(
                [
                    hidden[x][:, (2 * row + y) * depth : (2 * row + y + 1) * depth]
                    for x in range(2)
                    for y in range(2)
                ],
                axis=0,
            )
            sums = dot(rows, pairs)
            total = sums[:channels]
            for piece in range(1, 4):
                total = total + sums[piece * channels : (piece + 1) * channels]
            pooled_ref[:, row * low_depth : (row + 1) * low_depth] = (0.125 * total).astype(BF16)

    pooled, slope, whole = call(
        first_kernel,
        (
            shaped((channels, low_cells), BF16),
            shaped((planes, channels, fine_cells), F32),
            shaped((planes + 2, channels, fine_cells), BF16),
        ),
        (pltpu.VMEM((9 * channels, 3 * channels), BF16),),
    )(*own, *side_a, *side_b, first_weight)

    pool_d = along(pooled, table_d)
    pool_x = along(pooled, mirror(2))
    pool_a = along(pooled, mirror(1))
    pool_ax = along(pool_x, mirror(1))
    pool_ad = along(pool_d, mirror(1))

    def matrix_kernel(*refs):
        narrow_refs, taps = refs[:filt], refs[filt]
        forward_ref, back_ref, first_ref = refs[filt + 1 :]
        for slot, ref in enumerate(narrow_refs):
            values = [ref[t, :, :64] if t < 14 else ref[t - 13, :, 64:] for t in range(27)]
            forward_matrix(values, forward_ref.at[slot], filters)
            back_ref[slot] = backward_matrix(values)
        first_ref[...] = backward_matrix([taps[t] for t in range(27)])

    second_forward, second_back, first_back = call(
        matrix_kernel,
        (
            shaped((filt, 9 * filters, 3 * channels), BF16),
            shaped((filt, 9 * channels, 3 * filters), BF16),
            shaped((9 * channels, 3 * channels), BF16),
        ),
    )(*narrows, first_weight)

    first_rows, second_rows = 9 * channels, 9 * filters
    packed_first, packed_second = first_rows * 3 // 2, second_rows * 3 // 2
    far_side = space // 4
    unit = 8 * space
    total_rows = -(-(packed_first + packed_second) // unit) * unit
    half = total_rows // 2
    chunk = half // far_side

    def middle_kernel(*refs):
        own_refs, a_refs, b_refs = refs[:filt], refs[filt : 2 * filt], refs[2 * filt : 3 * filt]
        pool_ref, pa_ref, px_ref, pd_ref, pax_ref, pad_ref = refs[3 * filt : 3 * filt + 6]
        forward_ref, back_ref, slope_ref, whole_ref = refs[3 * filt + 6 : 3 * filt + 10]
        features_ref, down_ref, edge_a_ref, edge_b_ref, keep_ref, send_ref = refs[
            3 * filt + 10 : 3 * filt + 16
        ]
        first_acc, second_acc, rows_ref, parts_ref = refs[3 * filt + 16 :]
        index = lax.axis_index("space")
        odd = index % 2 == 1
        up = (index // 2) % 2 == 1
        inside = jnp.logical_and(index > 0, index < space - 1)
        inside_two = jnp.logical_and(index > 1, index < space - 2)
        blank = jnp.zeros((channels, low_cells), BF16)
        got_d = pick(inside_two, pd_ref[...], blank)
        got_ad = pick(inside_two, pad_ref[...], blank)
        got_a, got_x, got_ax = pa_ref[...], px_ref[...], pax_ref[...]
        other = pick(odd == up, got_ad, got_ax)
        pools = [
            pick(up, got_x, got_d),
            pick(odd, got_a, other),
            pool_ref[...],
            pick(odd, other, got_a),
            pick(up, got_d, got_x),
        ]
        stacks = [stack3(value, low_depth) for value in pools]

        def cot_of(packed):
            return jnp.concatenate(
                [packed[k * filters : (k + 1) * filters] for k in range(blocks)], axis=1
            ).astype(F32)

        for slot in range(filt):
            pre = conv_planes(forward_ref.at[slot], stacks, 3, filters, low_depth)
            cot_own = cot_of(own_refs[slot][:, planes * brick :])
            cot_a = cot_of(a_refs[slot][:, planes * brick :])
            cot_b = cot_of(b_refs[slot][:, brick:])
            cot_b = pick(inside, cot_b, jnp.zeros_like(cot_b))
            cots = [pick(odd, cot_a, cot_b), cot_own, pick(odd, cot_b, cot_a)]
            downs = [
                (value * silu_slope(pre[plane])).astype(BF16) for plane, value in enumerate(cots)
            ]
            if slot == 0:
                features_ref[...] = silu(pre[1]).astype(BF16)
                weight_planes(second_acc, [downs[1]], stacks[1:4], low_depth)
            down_stacks = [stack3(value, low_depth) for value in downs]
            (part,) = conv_planes(back_ref.at[slot], down_stacks, 1, channels, low_depth)
            parts_ref[lax.axis_index("filt") ^ slot] = part.astype(BF16)

        spread = (
            lax.broadcasted_iota(jnp.int32, (low_depth, depth), 0)
            == lax.broadcasted_iota(jnp.int32, (low_depth, depth), 1) // 2
        ).astype(BF16)
        columns = []
        for row in range(low_y):
            wide = None
            for group in range(filt):
                cells = parts_ref[group, :, row * low_depth : (row + 1) * low_depth]
                term = dot(cells, spread)
                wide = term if wide is None else wide + term
            columns += [0.125 * wide] * 2
        hidden_grad = jnp.concatenate(columns, axis=1)
        grads = [(hidden_grad * slope_ref[p]).astype(BF16) for p in range(planes)]
        for plane in range(planes):
            down_ref[plane] = grads[plane]
        edge_a_ref[...] = pick(odd, grads[0], grads[planes - 1])
        edge_b_ref[...] = pick(odd, grads[planes - 1], grads[0])
        fine_stacks = [stack3(whole_ref[p], depth) for p in range(planes + 2)]
        weight_planes(first_acc, grads, fine_stacks, depth)
        pack(first_acc, rows_ref, 0, first_rows)
        pack(second_acc, rows_ref, packed_first, second_rows)
        if total_rows > packed_first + packed_second:
            rows_ref[packed_first + packed_second :, :] = jnp.zeros(
                (total_rows - packed_first - packed_second, 128), F32
            )
        core = index % 2
        keep_ref[...] = rows_ref[pl.ds(pl.multiple_of(core * half, 16), half), :]
        send_ref[...] = rows_ref[pl.ds(pl.multiple_of((1 - core) * half, 16), half), :].astype(
            BF16
        )

    features, first_down, edge_a, edge_b, keep, send = call(
        middle_kernel,
        (
            shaped((filters, low_cells), BF16),
            shaped((planes, channels, fine_cells), BF16),
            shaped((channels, fine_cells), BF16),
            shaped((channels, fine_cells), BF16),
            shaped((half, 128), F32),
            shaped((half, 128), BF16),
        ),
        (
            pltpu.VMEM((first_rows, 3 * channels), F32),
            pltpu.VMEM((second_rows, 3 * channels), F32),
            pltpu.VMEM((total_rows, 128), F32),
            pltpu.VMEM((filt, channels, low_cells), BF16),
        ),
    )(
        *own,
        *side_a,
        *side_b,
        pooled,
        pool_a,
        pool_x,
        pool_d,
        pool_ax,
        pool_ad,
        second_forward,
        second_back,
        slope,
        whole,
    )
    features = features.reshape(filters, 1, low_y, low_depth)

    got = along(send, mirror(1))

    def split_kernel(keep_ref, got_ref, *refs):
        out_refs, rows_ref = refs[:-1], refs[-1]
        rows_ref[...] = keep_ref[...] + got_ref[...].astype(F32)
        high = lax.axis_index("space") // 4
        out_refs[0][...] = rows_ref[pl.ds(pl.multiple_of(high * chunk, 16), chunk), :]
        for k in range(1, far_side):
            start = pl.multiple_of((high ^ k) * chunk, 16)
            out_refs[k][...] = rows_ref[pl.ds(start, chunk), :].astype(BF16)

    own_chunk, *sends = call(
        split_kernel,
        (shaped((chunk, 128), F32),) + (shaped((chunk, 128), BF16),) * (far_side - 1),
        (pltpu.VMEM((half, 128), F32),),
    )(keep, got)
    got = [along(sends[k - 1], mirror(4 * k)) for k in range(1, far_side)]
    halo_a, halo_b = along(edge_a, mirror(1)), along(edge_b, table_b)

    def sum_kernel(own_ref, *refs):
        total = own_ref[...].astype(F32)
        for ref in refs[:-1]:
            total = total + ref[...].astype(F32)
        refs[-1][...] = total.astype(BF16)

    summed = call(sum_kernel, shaped((chunk, 128), BF16))(own_chunk, *got)
    other = along(summed, mirror(2))

    def volume_kernel(own_ref, a_ref, b_ref, matrices, out_ref, rows_ref):
        index = lax.axis_index("space")
        odd = index % 2 == 1
        inside = jnp.logical_and(index > 0, index < space - 1)
        got_a, got_b = a_ref[...], b_ref[...]
        got_b = pick(inside, got_b, jnp.zeros_like(got_b))
        values = [pick(odd, got_a, got_b)] + [own_ref[p] for p in range(planes)]
        values.append(pick(odd, got_b, got_a))
        blank = jnp.zeros((channels, depth), BF16)
        begin = pl.multiple_of(lax.axis_index("filt") * brick, brick)
        stacks = []
        for position, value in enumerate(values):
            rows_ref[position] = jnp.concatenate([blank, value, blank], axis=1)
            stacks.append(stack3(rows_ref[position, :, pl.ds(begin, brick + 2 * depth)], depth))
        results = conv_planes(matrices, stacks, planes, channels, depth)
        for plane in range(planes):
            out_ref[plane] = results[plane][:, depth : depth + brick].astype(BF16)

    volume_grad = call(
        volume_kernel,
        shaped((planes, channels, brick), BF16),
        (pltpu.VMEM((planes + 2, channels, fine_cells + 2 * depth), BF16),),
    )(first_down, halo_a, halo_b, first_back)
    volume_grad = jnp.transpose(volume_grad.reshape(planes, channels, brick_y, depth), (1, 0, 2, 3))

    final_chunk = call(sum_kernel, shaped((chunk, 128), BF16))(summed, other)
    pieces = [final_chunk] + [along(final_chunk, mirror(4 * k)) for k in range(1, far_side)]

    def join_kernel(*refs):
        high = lax.axis_index("space") // 4
        for k, ref in enumerate(refs[:-1]):
            refs[-1][pl.ds(pl.multiple_of((high ^ k) * chunk, 16), chunk), :] = ref[...]

    group = call(join_kernel, shaped((half, 128), BF16))(*pieces)
    partner = along(group, mirror(1))

    def final_kernel(own_ref, got_ref, first_ref, second_ref, rows_ref):
        core = lax.axis_index("space") % 2
        rows_ref[pl.ds(pl.multiple_of(core * half, 16), half), :] = own_ref[...].astype(F32)
        rows_ref[pl.ds(pl.multiple_of((1 - core) * half, 16), half), :] = got_ref[...].astype(F32)
        unpack(rows_ref, 0, first_rows, first_ref, fine_scale)
        unpack(rows_ref, packed_first, second_rows, second_ref, low_scale)

    first_grad, second_grad = call(
        final_kernel,
        (
            jax.ShapeDtypeStruct((27, channels, channels), F32),
            jax.ShapeDtypeStruct((27, filters, channels), F32),
        ),
        (pltpu.VMEM((total_rows, 128), F32),),
    )(group, partner)
    return (features, volume_grad, first_grad, second_grad)


def solution(mesh):
    def whole_program(*args):
        return local(mesh.shape["space"], mesh.shape["filt"], *args)

    placed = (
        P(None, "space", "filt", None),
        P(),
        P(None, "filt", None),
        P("filt", "space", None, None),
    )
    return jax.shard_map(
        whole_program,
        mesh=mesh,
        in_specs=placed,
        out_specs=(
            P("filt", "space", None, None),
            P(None, "space", "filt", None),
            P(),
            P(None, "filt", None),
        ),
        check_vma=False,
    )
```

```python
import jax
import jax.numpy as jnp
from jax import lax
from jax.experimental import pallas as pl
from jax.experimental.pallas import tpu as pltpu
from jax.sharding import PartitionSpec as P


F32 = jnp.float32
BF16 = jnp.bfloat16
VMEM_LIMIT = 32 * 1024 * 1024


def call(body, outs, scratch=(), far=(), aliases=None, out_far=False):
    def run(*args):
        kernel = pl.pallas_call(
            body,
            out_shape=outs,
            in_specs=[
                pl.BlockSpec(memory_space=pltpu.HBM if k in far else pltpu.VMEM)
                for k in range(len(args))
            ],
            out_specs=jax.tree.map(
                lambda _: pl.BlockSpec(memory_space=pltpu.HBM if out_far else pltpu.VMEM), outs
            ),
            scratch_shapes=scratch,
            input_output_aliases=aliases or {},
            compiler_params=pltpu.CompilerParams(vmem_limit_bytes=VMEM_LIMIT),
        )
        near = [
            pltpu.with_memory_space_constraint(arg, pltpu.HBM if k in far else pltpu.VMEM)
            for k, arg in enumerate(args)
        ]
        return kernel(*near)

    return run


def shaped(shape, dtype):
    return pltpu.VMEM(shape, dtype)


def dot(lhs, rhs):
    return jnp.dot(lhs, rhs, preferred_element_type=F32)


def dot_cells(lhs, rhs):
    return lax.dot_general(lhs, rhs, (((1,), (1,)), ((), ())), preferred_element_type=F32)


def silu_slope(values):
    part = 1.0 / (1.0 + jnp.exp(-values))
    return part * (1.0 + values * (1.0 - part))


def silu(values):
    return values / (1.0 + jnp.exp(-values))


def stack3(cells, depth):
    count = cells.shape[1]
    lane = lax.broadcasted_iota(jnp.int32, cells.shape, 1) % depth
    wide = cells.astype(F32)
    below = jnp.where(lane == 0, 0.0, pltpu.roll(wide, 1, 1)).astype(BF16)
    above = jnp.where(lane == depth - 1, 0.0, pltpu.roll(wide, count - 1, 1)).astype(BF16)
    return jnp.concatenate([below, cells, above], axis=0)


def shifted_rows(cells, offset, depth):
    if offset == 0:
        return cells
    blank = jnp.zeros((cells.shape[0], depth), cells.dtype)
    if cells.shape[1] == depth:
        return blank
    if offset > 0:
        return jnp.concatenate([cells[:, depth:], blank], axis=1)
    return jnp.concatenate([blank, cells[:, :-depth]], axis=1)


def conv_planes(matrices, stacks, planes, outputs, depth, results=None):
    results = list(results) if results else [None] * planes
    for place, stack in stacks.items():
        first = max(0, place - planes + 1)
        last = min(2, place)
        rows = matrices[first * 3 * outputs : (last + 1) * 3 * outputs, :]
        terms = dot(rows, stack)
        for tap_x in range(first, last + 1):
            for tap_y in range(3):
                begin = ((tap_x - first) * 3 + tap_y) * outputs
                term = shifted_rows(terms[begin : begin + outputs], tap_y - 1, depth)
                target = place - tap_x
                results[target] = term if results[target] is None else results[target] + term
    return results


def weight_planes(grads, stacks, depth):
    planes = len(grads)
    rows = [
        jnp.concatenate([shifted_rows(grad, 1 - tap_y, depth) for tap_y in range(3)], axis=0)
        for grad in grads
    ]
    sums = []
    for tap_x in range(3):
        total = None
        for plane in range(planes):
            term = dot_cells(rows[plane], stacks[plane + tap_x])
            total = term if total is None else total + term
        sums.append(total)
    return sums


def packed(sums, count):
    acc = jnp.concatenate(sums, axis=0)
    rows = acc.shape[0]
    tail = jnp.concatenate([acc[: rows // 2, 128:], acc[rows // 2 :, 128:]], axis=1)
    pieces = [acc[:, :128], tail]
    if count > rows * 3 // 2:
        pieces.append(jnp.zeros((count - rows * 3 // 2, 128), F32))
    return jnp.concatenate(pieces, axis=0)


def unpack(source, base, rows, out, scale):
    half = rows // 2
    outputs = rows // 9
    for pair in range(9):
        main = source[base + pair * outputs : base + (pair + 1) * outputs, :].astype(F32) * scale
        out[3 * pair] = main[:, :64]
        out[3 * pair + 1] = main[:, 64:]
    for piece in range(0, 9 * outputs, 8):
        row = piece if piece < half else piece - half
        tail = source[base + rows + row : base + rows + row + 8, :].astype(F32) * scale
        side = tail[:, :64] if piece < half else tail[:, 64:]
        out[3 * (piece // outputs) + 2, piece % outputs : piece % outputs + 8, :] = side


def forward_matrix(taps, target, outputs):
    for pair in range(9):
        target[pair * outputs : (pair + 1) * outputs, :] = jnp.concatenate(
            [taps[3 * pair + tap_z] for tap_z in range(3)], axis=1
        )


def backward_matrix(taps):
    rows = [
        jnp.concatenate([taps[26 - 3 * pair - tap_z] for pair in range(9)], axis=1)
        for tap_z in range(3)
    ]
    return jnp.concatenate(rows, axis=0).T


def pick(flag, one, other):
    return jnp.where(flag, one, other)


def swap_tables(count):
    ends = [(0, 0), (count - 1, count - 1)]
    table_b = ends + [(i, i + 1) for i in range(1, count - 1, 2)]
    table_b += [(i + 1, i) for i in range(1, count - 1, 2)]
    low = [i for i in range(count - 2) if i % 4 >= 2]
    table_d = [(i, i + 2) for i in low] + [(i + 2, i) for i in low]
    table_d += [(0, 0), (1, 1), (count - 2, count - 2), (count - 1, count - 1)]
    return table_b, table_d


def join_rows(target, place, pieces, brick):
    index = lax.axis_index("filt")
    for slot, piece in enumerate(pieces):
        start = pl.multiple_of((index ^ slot) * brick, brick)
        target[place, :, pl.ds(start, brick)] = piece


def local(space, filt, volume, first_weight, second_weight, cotangent):
    channels, planes, brick_y, depth = volume.shape
    filters = second_weight.shape[1]
    fine_y = brick_y * filt
    low_y = fine_y // 2
    low_depth = depth // 2
    fine_cells = fine_y * depth
    low_cells = low_y * low_depth
    brick = brick_y * depth
    fine_scale = 1.0 / (planes * space * fine_cells) ** 0.5
    low_scale = 1.0 / (planes // 2 * space * low_cells) ** 0.5
    blocks = channels // filters
    extra = low_cells // blocks
    table_b, table_d = swap_tables(space)

    def mirror(mask):
        return [(i, i ^ mask) for i in range(space)]

    def along(piece, table):
        return lax.ppermute(piece, "space", table)

    def across(piece, table, slot):
        pairs = [(i * filt + f, j * filt + (f ^ slot)) for i, j in table for f in range(filt)]
        return lax.ppermute(piece, ("space", "filt"), pairs)


    def message_kernel(*refs):
        far_refs, own_ref, edge_ref, narrow_ref, first_ref = refs[:4], *refs[4:8]
        cells_ref, cot_ref, second_ref, sems = refs[8:]
        odd = lax.axis_index("space") % 2 == 1
        copies = [
            pltpu.make_async_copy(source, target, sems.at[k])
            for k, (source, target) in enumerate(
                zip(far_refs, (cells_ref, cot_ref, second_ref, first_ref))
            )
        ]
        for copy in copies:
            copy.start()
        copies[0].wait()
        for plane in range(planes):
            for row in range(brick_y):
                start = (plane * brick_y + row) * depth
                own_ref[:, start : start + depth] = cells_ref[:, plane, row, :]
        copies[1].wait()
        width = low_y // blocks
        for row in range(low_y):
            block, start = row // width, (row % width) * low_depth
            piece = cot_ref[:, 0, row, :]
            own_ref[
                block * filters : (block + 1) * filters,
                planes * brick + start : planes * brick + start + low_depth,
            ] = piece
        edge_ref[:, :brick] = pick(
            odd, own_ref[:, (planes - 1) * brick : planes * brick], own_ref[:, :brick]
        )
        edge_ref[:, brick:] = own_ref[:, planes * brick :]

        copies[2].wait()
        for tap in range(14):
            narrow_ref[tap] = jnp.concatenate([second_ref[tap], second_ref[tap + 13]], axis=1)
        copies[3].wait()

    own_message, edge_message, narrow, first_taps = call(
        message_kernel,
        (
            shaped((channels, planes * brick + extra), BF16),
            shaped((channels, brick + extra), BF16),
            shaped((14, filters, 128), BF16),
            shaped(first_weight.shape, BF16),
        ),
        (
            pltpu.VMEM(volume.shape, BF16),
            pltpu.VMEM(cotangent.shape, BF16),
            pltpu.VMEM(second_weight.shape, BF16),
            pltpu.SemaphoreType.DMA((4,)),
        ),
        far=(0, 1, 2, 3),
    )(volume, cotangent, second_weight, first_weight)
    own = [own_message] + [across(own_message, mirror(0), slot) for slot in range(1, filt)]
    side_b = [across(edge_message, table_b, slot) for slot in range(filt)]
    side_a = [along(message, mirror(1)) for message in own]

    narrows = [narrow] + [across(narrow, mirror(0), slot) for slot in range(1, filt)]

    def own_kernel(*refs):
        own_refs, taps = refs[:filt], refs[filt]
        whole_ref, sums_ref, matrices = refs[filt + 1 :]
        forward_matrix(taps, matrices, channels)
        for plane in range(planes):
            pieces = [ref[:, plane * brick : (plane + 1) * brick] for ref in own_refs]
            join_rows(whole_ref, plane, pieces, brick)
        stacks = {1 + plane: stack3(whole_ref[plane], depth) for plane in range(planes)}
        sums = conv_planes(matrices, stacks, planes, channels, depth)
        for plane in range(planes):
            sums_ref[plane] = sums[plane]

    whole, own_sums, first_forward = call(
        own_kernel,
        (
            shaped((planes, channels, fine_cells), BF16),
            shaped((planes, channels, fine_cells), F32),
            shaped((9 * channels, 3 * channels), BF16),
        ),
    )(*own, first_taps)

    def first_kernel(*refs):
        a_refs, b_refs = refs[:filt], refs[filt : 2 * filt]
        sums_ref, matrices, pooled_ref, slope_ref, sides_ref = refs[2 * filt :]
        index = lax.axis_index("space")
        odd = index % 2 == 1
        inside = jnp.logical_and(index > 0, index < space - 1)
        lefts, rights = [], []
        for a_ref, b_ref in zip(a_refs, b_refs):
            got_a = pick(odd, a_ref[:, (planes - 1) * brick : planes * brick], a_ref[:, :brick])
            got_b = b_ref[:, :brick]
            got_b = pick(inside, got_b, jnp.zeros_like(got_b))
            lefts.append(pick(odd, got_a, got_b))
            rights.append(pick(odd, got_b, got_a))
        join_rows(sides_ref, 0, lefts, brick)
        join_rows(sides_ref, 1, rights, brick)
        stacks = {0: stack3(sides_ref[0], depth), planes + 1: stack3(sides_ref[1], depth)}
        sums = [sums_ref[plane] for plane in range(planes)]
        pre = conv_planes(matrices, stacks, planes, channels, depth, sums)
        hidden = [silu(value).astype(BF16) for value in pre]
        for plane in range(planes):
            slope_ref[plane] = silu_slope(pre[plane])
        pairs = (
            lax.broadcasted_iota(jnp.int32, (depth, low_depth), 0) // 2
            == lax.broadcasted_iota(jnp.int32, (depth, low_depth), 1)
        ).astype(BF16)
        for row in range(low_y):
            rows = jnp.concatenate(
                [
                    hidden[x][:, (2 * row + y) * depth : (2 * row + y + 1) * depth]
                    for x in range(2)
                    for y in range(2)
                ],
                axis=0,
            )
            sums = dot(rows, pairs)
            total = sums[:channels]
            for piece in range(1, 4):
                total = total + sums[piece * channels : (piece + 1) * channels]
            pooled_ref[:, row * low_depth : (row + 1) * low_depth] = (0.125 * total).astype(BF16)

    pooled, slope, sides = call(
        first_kernel,
        (
            shaped((channels, low_cells), BF16),
            shaped((planes, channels, fine_cells), F32),
            shaped((2, channels, fine_cells), BF16),
        ),
    )(*side_a, *side_b, own_sums, first_forward)

    pool_d = along(pooled, table_d)
    pool_x = along(pooled, mirror(2))
    pool_a = along(pooled, mirror(1))
    pool_ax = along(pool_x, mirror(1))
    pool_ad = along(pool_d, mirror(1))

    def matrix_kernel(*refs):
        narrow_refs, taps, whole_ref, sides_ref = refs[:filt], refs[filt], refs[filt + 1], refs[filt + 2]
        forward_ref, back_ref, first_ref, fine_ref = refs[filt + 3 :]
        for slot, ref in enumerate(narrow_refs):
            values = [ref[t, :, :64] if t < 14 else ref[t - 13, :, 64:] for t in range(27)]
            forward_matrix(values, forward_ref.at[slot], filters)
            back_ref[slot] = backward_matrix(values)
        first_ref[...] = backward_matrix([taps[t] for t in range(27)])
        fine_ref[0] = stack3(sides_ref[0], depth)
        fine_ref[planes + 1] = stack3(sides_ref[1], depth)
        for plane in range(planes):
            fine_ref[1 + plane] = stack3(whole_ref[plane], depth)

    second_forward, second_back, first_back, fine_stacks = call(
        matrix_kernel,
        (
            shaped((filt, 9 * filters, 3 * channels), BF16),
            shaped((filt, 9 * channels, 3 * filters), BF16),
            shaped((9 * channels, 3 * channels), BF16),
            shaped((planes + 2, 3 * channels, fine_cells), BF16),
        ),
    )(*narrows, first_taps, whole, sides)

    first_rows, second_rows = 9 * channels, 9 * filters
    packed_first, packed_second = first_rows * 3 // 2, second_rows * 3 // 2
    far_side = space // 4
    unit = 16 * far_side
    half = -(-max(packed_first, packed_second) // unit) * unit
    chunk = half // far_side

    def middle_kernel(*refs):
        own_refs, a_refs, b_refs = refs[:filt], refs[filt : 2 * filt], refs[2 * filt : 3 * filt]
        pool_ref, pa_ref, px_ref, pd_ref, pax_ref, pad_ref = refs[3 * filt : 3 * filt + 6]
        forward_ref, back_ref, slope_ref, fine_ref = refs[3 * filt + 6 : 3 * filt + 10]
        features_ref, down_ref, edge_a_ref, edge_b_ref, keep_ref, send_ref = refs[
            3 * filt + 10 : 3 * filt + 16
        ]
        parts_ref = refs[3 * filt + 16]
        index = lax.axis_index("space")
        odd = index % 2 == 1
        up = (index // 2) % 2 == 1
        inside = jnp.logical_and(index > 0, index < space - 1)
        inside_two = jnp.logical_and(index > 1, index < space - 2)
        blank = jnp.zeros((channels, low_cells), BF16)
        got_d = pick(inside_two, pd_ref[...], blank)
        got_ad = pick(inside_two, pad_ref[...], blank)
        got_a, got_x, got_ax = pa_ref[...], px_ref[...], pax_ref[...]
        other = pick(odd == up, got_ad, got_ax)
        pools = [
            pick(up, got_x, got_d),
            pick(odd, got_a, other),
            pool_ref[...],
            pick(odd, other, got_a),
            pick(up, got_d, got_x),
        ]
        stacks = {k: stack3(value, low_depth) for k, value in enumerate(pools)}

        def cot_of(packed):
            return jnp.concatenate(
                [packed[k * filters : (k + 1) * filters] for k in range(blocks)], axis=1
            ).astype(F32)

        for slot in range(filt):
            pre = conv_planes(forward_ref.at[slot], stacks, 3, filters, low_depth)
            cot_own = cot_of(own_refs[slot][:, planes * brick :])
            cot_a = cot_of(a_refs[slot][:, planes * brick :])
            cot_b = cot_of(b_refs[slot][:, brick:])
            cot_b = pick(inside, cot_b, jnp.zeros_like(cot_b))
            cots = [pick(odd, cot_a, cot_b), cot_own, pick(odd, cot_b, cot_a)]
            downs = [
                (value * silu_slope(pre[plane])).astype(BF16) for plane, value in enumerate(cots)
            ]
            if slot == 0:
                features_ref[...] = silu(pre[1]).astype(BF16)
                second_sums = weight_planes([downs[1]], [stacks[1], stacks[2], stacks[3]], low_depth)
            down_stacks = {k: stack3(value, low_depth) for k, value in enumerate(downs)}
            (part,) = conv_planes(back_ref.at[slot], down_stacks, 1, channels, low_depth)
            parts_ref[lax.axis_index("filt") ^ slot] = part.astype(BF16)

        spread = (
            lax.broadcasted_iota(jnp.int32, (low_depth, depth), 0)
            == lax.broadcasted_iota(jnp.int32, (low_depth, depth), 1) // 2
        ).astype(BF16)
        columns = []
        for row in range(low_y):
            wide = None
            for group in range(filt):
                cells = parts_ref[group, :, row * low_depth : (row + 1) * low_depth]
                term = dot(cells, spread)
                wide = term if wide is None else wide + term
            columns += [0.125 * wide] * 2
        hidden_grad = jnp.concatenate(columns, axis=1)
        grads = [(hidden_grad * slope_ref[p]).astype(BF16) for p in range(planes)]
        for plane in range(planes):
            down_ref[plane] = grads[plane]
        edge_a_ref[...] = pick(odd, grads[0], grads[planes - 1])
        edge_b_ref[...] = pick(odd, grads[planes - 1], grads[0])
        fine_stacks = [fine_ref[p] for p in range(planes + 2)]
        first_sums = packed(weight_planes(grads, fine_stacks, depth), half)
        second_sums = packed(second_sums, half)
        keep_ref[...] = pick(odd, second_sums, first_sums)
        send_ref[...] = pick(odd, first_sums, second_sums).astype(BF16)

    flat_features, first_down, edge_a, edge_b, keep, send = call(
        middle_kernel,
        (
            shaped((filters, low_cells), BF16),
            shaped((planes, channels, fine_cells), BF16),
            shaped((channels, fine_cells), BF16),
            shaped((channels, fine_cells), BF16),
            shaped((half, 128), F32),
            shaped((half, 128), BF16),
        ),
        (
            pltpu.VMEM((filt, channels, low_cells), BF16),
        ),
    )(
        *own,
        *side_a,
        *side_b,
        pooled,
        pool_a,
        pool_x,
        pool_d,
        pool_ax,
        pool_ad,
        second_forward,
        second_back,
        slope,
        fine_stacks,
    )

    got = along(send, mirror(1))

    def split_kernel(keep_ref, got_ref, *refs):
        out_refs, rows_ref = refs[:-1], refs[-1]
        rows_ref[...] = keep_ref[...] + got_ref[...].astype(F32)
        high = lax.axis_index("space") // 4
        out_refs[0][...] = rows_ref[pl.ds(pl.multiple_of(high * chunk, 16), chunk), :]
        for k in range(1, far_side):
            start = pl.multiple_of((high ^ k) * chunk, 16)
            out_refs[k][...] = rows_ref[pl.ds(start, chunk), :].astype(BF16)

    own_chunk, *sends = call(
        split_kernel,
        (shaped((chunk, 128), F32),) + (shaped((chunk, 128), BF16),) * (far_side - 1),
        (pltpu.VMEM((half, 128), F32),),
    )(keep, got)
    got = [along(sends[k - 1], mirror(4 * k)) for k in range(1, far_side)]
    halo_a, halo_b = along(edge_a, mirror(1)), along(edge_b, table_b)

    def sum_kernel(own_ref, *refs):
        total = own_ref[...].astype(F32)
        for ref in refs[:-1]:
            total = total + ref[...].astype(F32)
        refs[-1][...] = total.astype(BF16)

    summed = call(sum_kernel, shaped((chunk, 128), BF16))(own_chunk, *got)
    other = along(summed, mirror(2))

    def volume_kernel(own_ref, a_ref, b_ref, matrices, flat_ref, out_ref, features_ref, rows_ref):
        index = lax.axis_index("space")
        odd = index % 2 == 1
        inside = jnp.logical_and(index > 0, index < space - 1)
        got_a, got_b = a_ref[...], b_ref[...]
        got_b = pick(inside, got_b, jnp.zeros_like(got_b))
        values = [pick(odd, got_a, got_b)] + [own_ref[p] for p in range(planes)]
        values.append(pick(odd, got_b, got_a))
        blank = jnp.zeros((channels, depth), BF16)
        begin = pl.multiple_of(lax.axis_index("filt") * brick, brick)
        stacks = {}
        for position, value in enumerate(values):
            rows_ref[position] = jnp.concatenate([blank, value, blank], axis=1)
            cells = rows_ref[position, :, pl.ds(begin, brick + 2 * depth)]
            stacks[position] = stack3(cells, depth)
        results = conv_planes(matrices, stacks, planes, channels, depth)
        for plane in range(planes):
            for row in range(brick_y):
                cells = results[plane][:, (row + 1) * depth : (row + 2) * depth]
                out_ref[:, plane, row, :] = cells.astype(BF16)
        for row in range(low_y):
            features_ref[:, 0, row, :] = flat_ref[:, row * low_depth : (row + 1) * low_depth]

    volume_grad, features = call(
        volume_kernel,
        (
            jax.ShapeDtypeStruct(volume.shape, BF16),
            jax.ShapeDtypeStruct(cotangent.shape, BF16),
        ),
        (pltpu.VMEM((planes + 2, channels, fine_cells + 2 * depth), BF16),),
    )(first_down, halo_a, halo_b, first_back, flat_features)

    final_chunk = call(sum_kernel, shaped((chunk, 128), BF16))(summed, other)
    pieces = [final_chunk] + [along(final_chunk, mirror(4 * k)) for k in range(1, far_side)]

    def join_kernel(*refs):
        high = lax.axis_index("space") // 4
        for k, ref in enumerate(refs[:-1]):
            refs[-1][pl.ds(pl.multiple_of((high ^ k) * chunk, 16), chunk), :] = ref[...]

    group = call(join_kernel, shaped((half, 128), BF16))(*pieces)
    partner = along(group, mirror(1))

    def final_kernel(own_ref, got_ref, first_ref, second_ref, rows_ref):
        core = lax.axis_index("space") % 2
        rows_ref[pl.ds(pl.multiple_of(core * half, 16), half), :] = own_ref[...].astype(F32)
        rows_ref[pl.ds(pl.multiple_of((1 - core) * half, 16), half), :] = got_ref[...].astype(F32)
        unpack(rows_ref, 0, first_rows, first_ref, fine_scale)
        unpack(rows_ref, half, second_rows, second_ref, low_scale)

    first_grad, second_grad = call(
        final_kernel,
        (
            jax.ShapeDtypeStruct((27, channels, channels), F32),
            jax.ShapeDtypeStruct((27, filters, channels), F32),
        ),
        (pltpu.VMEM((2 * half, 128), F32),),
    )(group, partner)
    return (features, volume_grad, first_grad, second_grad)


def solution(mesh):
    def whole_program(*args):
        return local(mesh.shape["space"], mesh.shape["filt"], *args)

    placed = (
        P(None, "space", "filt", None),
        P(),
        P(None, "filt", None),
        P("filt", "space", None, None),
    )
    return jax.shard_map(
        whole_program,
        mesh=mesh,
        in_specs=placed,
        out_specs=(
            P("filt", "space", None, None),
            P(None, "space", "filt", None),
            P(),
            P(None, "filt", None),
        ),
        check_vma=False,
    )
```

```python
import jax
import jax.numpy as jnp
from jax import lax
from jax.experimental import pallas as pl
from jax.experimental.pallas import tpu as pltpu
from jax.sharding import PartitionSpec as P


F32 = jnp.float32
BF16 = jnp.bfloat16
VMEM_LIMIT = 32 * 1024 * 1024


def call(body, outs, scratch=(), far=(), aliases=None, out_far=False):
    def run(*args):
        kernel = pl.pallas_call(
            body,
            out_shape=outs,
            in_specs=[
                pl.BlockSpec(memory_space=pltpu.HBM if k in far else pltpu.VMEM)
                for k in range(len(args))
            ],
            out_specs=jax.tree.map(
                lambda _: pl.BlockSpec(memory_space=pltpu.HBM if out_far else pltpu.VMEM), outs
            ),
            scratch_shapes=scratch,
            input_output_aliases=aliases or {},
            compiler_params=pltpu.CompilerParams(vmem_limit_bytes=VMEM_LIMIT),
        )
        near = [
            pltpu.with_memory_space_constraint(arg, pltpu.HBM if k in far else pltpu.VMEM)
            for k, arg in enumerate(args)
        ]
        return kernel(*near)

    return run


def shaped(shape, dtype):
    return pltpu.VMEM(shape, dtype)


def dot(lhs, rhs):
    return jnp.dot(lhs, rhs, preferred_element_type=F32)


def dot_cells(lhs, rhs):
    return lax.dot_general(lhs, rhs, (((1,), (1,)), ((), ())), preferred_element_type=F32)


def silu_slope(values):
    part = 1.0 / (1.0 + jnp.exp(-values))
    return part * (1.0 + values * (1.0 - part))


def silu(values):
    return values / (1.0 + jnp.exp(-values))


def stack3(cells, depth):
    count = cells.shape[1]
    lane = lax.broadcasted_iota(jnp.int32, cells.shape, 1) % depth
    wide = cells.astype(F32)
    below = jnp.where(lane == 0, 0.0, pltpu.roll(wide, 1, 1)).astype(BF16)
    above = jnp.where(lane == depth - 1, 0.0, pltpu.roll(wide, count - 1, 1)).astype(BF16)
    return jnp.concatenate([below, cells, above], axis=0)


def shifted_rows(cells, offset, depth):
    if offset == 0:
        return cells
    blank = jnp.zeros((cells.shape[0], depth), cells.dtype)
    if cells.shape[1] == depth:
        return blank
    if offset > 0:
        return jnp.concatenate([cells[:, depth:], blank], axis=1)
    return jnp.concatenate([blank, cells[:, :-depth]], axis=1)


def conv_planes(matrices, stacks, planes, outputs, depth, results=None):
    results = list(results) if results else [None] * planes
    for place, stack in stacks.items():
        first = max(0, place - planes + 1)
        last = min(2, place)
        rows = matrices[first * 3 * outputs : (last + 1) * 3 * outputs, :]
        terms = dot(rows, stack)
        for tap_x in range(first, last + 1):
            for tap_y in range(3):
                begin = ((tap_x - first) * 3 + tap_y) * outputs
                term = shifted_rows(terms[begin : begin + outputs], tap_y - 1, depth)
                target = place - tap_x
                results[target] = term if results[target] is None else results[target] + term
    return results


def weight_planes(grads, stacks, depth):
    planes = len(grads)
    rows = [
        jnp.concatenate([shifted_rows(grad, 1 - tap_y, depth) for tap_y in range(3)], axis=0)
        for grad in grads
    ]
    sums = []
    for tap_x in range(3):
        total = None
        for plane in range(planes):
            term = dot_cells(rows[plane], stacks[plane + tap_x])
            total = term if total is None else total + term
        sums.append(total)
    return sums


def packed(sums, count):
    acc = jnp.concatenate(sums, axis=0)
    rows = acc.shape[0]
    tail = jnp.concatenate([acc[: rows // 2, 128:], acc[rows // 2 :, 128:]], axis=1)
    pieces = [acc[:, :128], tail]
    if count > rows * 3 // 2:
        pieces.append(jnp.zeros((count - rows * 3 // 2, 128), F32))
    return jnp.concatenate(pieces, axis=0)


def unpack(source, base, rows, out, scale):
    half = rows // 2
    outputs = rows // 9
    for pair in range(9):
        main = source[base + pair * outputs : base + (pair + 1) * outputs, :].astype(F32) * scale
        out[3 * pair] = main[:, :64]
        out[3 * pair + 1] = main[:, 64:]
    for piece in range(0, 9 * outputs, 8):
        row = piece if piece < half else piece - half
        tail = source[base + rows + row : base + rows + row + 8, :].astype(F32) * scale
        side = tail[:, :64] if piece < half else tail[:, 64:]
        out[3 * (piece // outputs) + 2, piece % outputs : piece % outputs + 8, :] = side


def forward_matrix(taps, target, outputs):
    for pair in range(9):
        target[pair * outputs : (pair + 1) * outputs, :] = jnp.concatenate(
            [taps[3 * pair + tap_z] for tap_z in range(3)], axis=1
        )


def backward_matrix(taps):
    rows = [
        jnp.concatenate([taps[26 - 3 * pair - tap_z] for pair in range(9)], axis=1)
        for tap_z in range(3)
    ]
    return jnp.concatenate(rows, axis=0).T


def pick(flag, one, other):
    return jnp.where(flag, one, other)


def swap_tables(count):
    ends = [(0, 0), (count - 1, count - 1)]
    table_b = ends + [(i, i + 1) for i in range(1, count - 1, 2)]
    table_b += [(i + 1, i) for i in range(1, count - 1, 2)]
    low = [i for i in range(count - 2) if i % 4 >= 2]
    table_d = [(i, i + 2) for i in low] + [(i + 2, i) for i in low]
    table_d += [(0, 0), (1, 1), (count - 2, count - 2), (count - 1, count - 1)]
    return table_b, table_d


def join_rows(target, place, pieces, brick):
    index = lax.axis_index("filt")
    for slot, piece in enumerate(pieces):
        start = pl.multiple_of((index ^ slot) * brick, brick)
        target[place, :, pl.ds(start, brick)] = piece


def local(space, filt, volume, first_weight, second_weight, cotangent):
    channels, planes, brick_y, depth = volume.shape
    filters = second_weight.shape[1]
    fine_y = brick_y * filt
    low_y = fine_y // 2
    low_depth = depth // 2
    fine_cells = fine_y * depth
    low_cells = low_y * low_depth
    brick = brick_y * depth
    fine_scale = 1.0 / (planes * space * fine_cells) ** 0.5
    low_scale = 1.0 / (planes // 2 * space * low_cells) ** 0.5
    blocks = channels // filters
    extra = low_cells // blocks
    table_b, table_d = swap_tables(space)

    def mirror(mask):
        return [(i, i ^ mask) for i in range(space)]

    def along(piece, table):
        return lax.ppermute(piece, "space", table)

    def across(piece, table, slot):
        pairs = [(i * filt + f, j * filt + (f ^ slot)) for i, j in table for f in range(filt)]
        return lax.ppermute(piece, ("space", "filt"), pairs)


    def message_kernel(*refs):
        far_refs, own_ref, edge_ref, narrow_ref, first_ref = refs[:4], *refs[4:8]
        cells_ref, cot_ref, second_ref, sems = refs[8:]
        odd = lax.axis_index("space") % 2 == 1
        copies = [
            pltpu.make_async_copy(source, target, sems.at[k])
            for k, (source, target) in enumerate(
                zip(far_refs, (cells_ref, cot_ref, second_ref, first_ref))
            )
        ]
        for copy in copies:
            copy.start()
        copies[0].wait()
        for plane in range(planes):
            for row in range(brick_y):
                start = (plane * brick_y + row) * depth
                own_ref[:, start : start + depth] = cells_ref[:, plane, row, :]
        copies[1].wait()
        width = low_y // blocks
        for row in range(low_y):
            block, start = row // width, (row % width) * low_depth
            piece = cot_ref[:, 0, row, :]
            own_ref[
                block * filters : (block + 1) * filters,
                planes * brick + start : planes * brick + start + low_depth,
            ] = piece
        edge_ref[:, :brick] = pick(
            odd, own_ref[:, (planes - 1) * brick : planes * brick], own_ref[:, :brick]
        )
        edge_ref[:, brick:] = own_ref[:, planes * brick :]

        copies[2].wait()
        for tap in range(14):
            narrow_ref[tap] = jnp.concatenate([second_ref[tap], second_ref[tap + 13]], axis=1)
        copies[3].wait()

    own_message, edge_message, narrow, first_taps = call(
        message_kernel,
        (
            shaped((channels, planes * brick + extra), BF16),
            shaped((channels, brick + extra), BF16),
            shaped((14, filters, 128), BF16),
            shaped(first_weight.shape, BF16),
        ),
        (
            pltpu.VMEM(volume.shape, BF16),
            pltpu.VMEM(cotangent.shape, BF16),
            pltpu.VMEM(second_weight.shape, BF16),
            pltpu.SemaphoreType.DMA((4,)),
        ),
        far=(0, 1, 2, 3),
    )(volume, cotangent, second_weight, first_weight)
    own = [own_message] + [across(own_message, mirror(0), slot) for slot in range(1, filt)]
    side_b = [across(edge_message, table_b, slot) for slot in range(filt)]
    side_a = [along(message, mirror(1)) for message in own]

    narrows = [narrow] + [across(narrow, mirror(0), slot) for slot in range(1, filt)]

    def own_kernel(*refs):
        own_refs, taps = refs[:filt], refs[filt]
        whole_ref, sums_ref, matrices = refs[filt + 1 :]
        forward_matrix(taps, matrices, channels)
        for plane in range(planes):
            pieces = [ref[:, plane * brick : (plane + 1) * brick] for ref in own_refs]
            join_rows(whole_ref, plane, pieces, brick)
        stacks = {1 + plane: stack3(whole_ref[plane], depth) for plane in range(planes)}
        sums = conv_planes(matrices, stacks, planes, channels, depth)
        for plane in range(planes):
            sums_ref[plane] = sums[plane]

    whole, own_sums, first_forward = call(
        own_kernel,
        (
            shaped((planes, channels, fine_cells), BF16),
            shaped((planes, channels, fine_cells), F32),
            shaped((9 * channels, 3 * channels), BF16),
        ),
    )(*own, first_taps)

    def first_kernel(*refs):
        a_refs, b_refs = refs[:filt], refs[filt : 2 * filt]
        sums_ref, matrices, pooled_ref, slope_ref, sides_ref = refs[2 * filt :]
        index = lax.axis_index("space")
        odd = index % 2 == 1
        inside = jnp.logical_and(index > 0, index < space - 1)
        lefts, rights = [], []
        for a_ref, b_ref in zip(a_refs, b_refs):
            got_a = pick(odd, a_ref[:, (planes - 1) * brick : planes * brick], a_ref[:, :brick])
            got_b = b_ref[:, :brick]
            got_b = pick(inside, got_b, jnp.zeros_like(got_b))
            lefts.append(pick(odd, got_a, got_b))
            rights.append(pick(odd, got_b, got_a))
        join_rows(sides_ref, 0, lefts, brick)
        join_rows(sides_ref, 1, rights, brick)
        stacks = {0: stack3(sides_ref[0], depth), planes + 1: stack3(sides_ref[1], depth)}
        sums = [sums_ref[plane] for plane in range(planes)]
        pre = conv_planes(matrices, stacks, planes, channels, depth, sums)
        hidden = [silu(value).astype(BF16) for value in pre]
        for plane in range(planes):
            slope_ref[plane] = silu_slope(pre[plane])
        pairs = (
            lax.broadcasted_iota(jnp.int32, (depth, low_depth), 0) // 2
            == lax.broadcasted_iota(jnp.int32, (depth, low_depth), 1)
        ).astype(BF16)
        for row in range(low_y):
            rows = jnp.concatenate(
                [
                    hidden[x][:, (2 * row + y) * depth : (2 * row + y + 1) * depth]
                    for x in range(2)
                    for y in range(2)
                ],
                axis=0,
            )
            sums = dot(rows, pairs)
            total = sums[:channels]
            for piece in range(1, 4):
                total = total + sums[piece * channels : (piece + 1) * channels]
            pooled_ref[:, row * low_depth : (row + 1) * low_depth] = (0.125 * total).astype(BF16)

    pooled, slope, sides = call(
        first_kernel,
        (
            shaped((channels, low_cells), BF16),
            shaped((planes, channels, fine_cells), F32),
            shaped((2, channels, fine_cells), BF16),
        ),
    )(*side_a, *side_b, own_sums, first_forward)

    pool_d = along(pooled, table_d)
    pool_x = along(pooled, mirror(2))
    pool_a = along(pooled, mirror(1))
    pool_ax = along(pool_x, mirror(1))
    pool_ad = along(pool_d, mirror(1))

    def matrix_kernel(*refs):
        narrow_refs, taps, whole_ref, sides_ref = refs[:filt], refs[filt], refs[filt + 1], refs[filt + 2]
        forward_ref, back_ref, first_ref, fine_ref = refs[filt + 3 :]
        for slot, ref in enumerate(narrow_refs):
            values = [ref[t, :, :64] if t < 14 else ref[t - 13, :, 64:] for t in range(27)]
            forward_matrix(values, forward_ref.at[slot], filters)
            back_ref[slot] = backward_matrix(values)
        first_ref[...] = backward_matrix([taps[t] for t in range(27)])
        fine_ref[0] = stack3(sides_ref[0], depth)
        fine_ref[planes + 1] = stack3(sides_ref[1], depth)
        for plane in range(planes):
            fine_ref[1 + plane] = stack3(whole_ref[plane], depth)

    second_forward, second_back, first_back, fine_stacks = call(
        matrix_kernel,
        (
            shaped((filt, 9 * filters, 3 * channels), BF16),
            shaped((filt, 9 * channels, 3 * filters), BF16),
            shaped((9 * channels, 3 * channels), BF16),
            shaped((planes + 2, 3 * channels, fine_cells), BF16),
        ),
    )(*narrows, first_taps, whole, sides)

    first_rows, second_rows = 9 * channels, 9 * filters
    packed_first, packed_second = first_rows * 3 // 2, second_rows * 3 // 2
    far_side = space // 4
    unit = 16 * far_side
    half = -(-max(packed_first, packed_second) // unit) * unit
    chunk = half // far_side

    def middle_kernel(*refs):
        own_refs, a_refs, b_refs = refs[:filt], refs[filt : 2 * filt], refs[2 * filt : 3 * filt]
        pool_ref, pa_ref, px_ref, pd_ref, pax_ref, pad_ref = refs[3 * filt : 3 * filt + 6]
        forward_ref, back_ref, slope_ref, fine_ref = refs[3 * filt + 6 : 3 * filt + 10]
        features_ref, down_ref, edge_a_ref, edge_b_ref, keep_ref, send_ref = refs[
            3 * filt + 10 : 3 * filt + 16
        ]
        parts_ref = refs[3 * filt + 16]
        index = lax.axis_index("space")
        odd = index % 2 == 1
        up = (index // 2) % 2 == 1
        inside = jnp.logical_and(index > 0, index < space - 1)
        inside_two = jnp.logical_and(index > 1, index < space - 2)
        blank = jnp.zeros((channels, low_cells), BF16)
        got_d = pick(inside_two, pd_ref[...], blank)
        got_ad = pick(inside_two, pad_ref[...], blank)
        got_a, got_x, got_ax = pa_ref[...], px_ref[...], pax_ref[...]
        other = pick(odd == up, got_ad, got_ax)
        pools = [
            pick(up, got_x, got_d),
            pick(odd, got_a, other),
            pool_ref[...],
            pick(odd, other, got_a),
            pick(up, got_d, got_x),
        ]
        stacks = {k: stack3(value, low_depth) for k, value in enumerate(pools)}

        def cot_of(packed):
            return jnp.concatenate(
                [packed[k * filters : (k + 1) * filters] for k in range(blocks)], axis=1
            ).astype(F32)

        for slot in range(filt):
            pre = conv_planes(forward_ref.at[slot], stacks, 3, filters, low_depth)
            cot_own = cot_of(own_refs[slot][:, planes * brick :])
            cot_a = cot_of(a_refs[slot][:, planes * brick :])
            cot_b = cot_of(b_refs[slot][:, brick:])
            cot_b = pick(inside, cot_b, jnp.zeros_like(cot_b))
            cots = [pick(odd, cot_a, cot_b), cot_own, pick(odd, cot_b, cot_a)]
            downs = [
                (value * silu_slope(pre[plane])).astype(BF16) for plane, value in enumerate(cots)
            ]
            if slot == 0:
                features_ref[...] = silu(pre[1]).astype(BF16)
                second_sums = weight_planes([downs[1]], [stacks[1], stacks[2], stacks[3]], low_depth)
            down_stacks = {k: stack3(value, low_depth) for k, value in enumerate(downs)}
            (part,) = conv_planes(back_ref.at[slot], down_stacks, 1, channels, low_depth)
            parts_ref[lax.axis_index("filt") ^ slot] = part.astype(BF16)

        spread = (
            lax.broadcasted_iota(jnp.int32, (low_depth, depth), 0)
            == lax.broadcasted_iota(jnp.int32, (low_depth, depth), 1) // 2
        ).astype(BF16)
        columns = []
        for row in range(low_y):
            wide = None
            for group in range(filt):
                cells = parts_ref[group, :, row * low_depth : (row + 1) * low_depth]
                term = dot(cells, spread)
                wide = term if wide is None else wide + term
            columns += [0.125 * wide] * 2
        hidden_grad = jnp.concatenate(columns, axis=1)
        grads = [(hidden_grad * slope_ref[p]).astype(BF16) for p in range(planes)]
        for plane in range(planes):
            down_ref[plane] = grads[plane]
        edge_a_ref[...] = pick(odd, grads[0], grads[planes - 1])
        edge_b_ref[...] = pick(odd, grads[planes - 1], grads[0])
        fine_stacks = [fine_ref[p] for p in range(planes + 2)]
        first_sums = packed(weight_planes(grads, fine_stacks, depth), half)
        second_sums = packed(second_sums, half)
        keep_ref[...] = pick(odd, second_sums, first_sums)
        send_ref[...] = pick(odd, first_sums, second_sums).astype(BF16)

    flat_features, first_down, edge_a, edge_b, keep, send = call(
        middle_kernel,
        (
            shaped((filters, low_cells), BF16),
            shaped((planes, channels, fine_cells), BF16),
            shaped((channels, fine_cells), BF16),
            shaped((channels, fine_cells), BF16),
            shaped((half, 128), F32),
            shaped((half, 128), BF16),
        ),
        (
            pltpu.VMEM((filt, channels, low_cells), BF16),
        ),
    )(
        *own,
        *side_a,
        *side_b,
        pooled,
        pool_a,
        pool_x,
        pool_d,
        pool_ax,
        pool_ad,
        second_forward,
        second_back,
        slope,
        fine_stacks,
    )

    got = along(send, mirror(1))

    def split_kernel(keep_ref, got_ref, *refs):
        out_refs, rows_ref = refs[:-1], refs[-1]
        rows_ref[...] = keep_ref[...] + got_ref[...].astype(F32)
        high = lax.axis_index("space") // 4
        out_refs[0][...] = rows_ref[pl.ds(pl.multiple_of(high * chunk, 16), chunk), :]
        for k in range(1, far_side):
            start = pl.multiple_of((high ^ k) * chunk, 16)
            out_refs[k][...] = rows_ref[pl.ds(start, chunk), :].astype(BF16)

    own_chunk, *sends = call(
        split_kernel,
        (shaped((chunk, 128), F32),) + (shaped((chunk, 128), BF16),) * (far_side - 1),
        (pltpu.VMEM((half, 128), F32),),
    )(keep, got)
    got = [along(sends[k - 1], mirror(4 * k)) for k in range(1, far_side)]
    halo_a, halo_b = along(edge_a, mirror(1)), along(edge_b, table_b)

    def sum_kernel(own_ref, *refs):
        total = own_ref[...].astype(F32)
        for ref in refs[:-1]:
            total = total + ref[...].astype(F32)
        refs[-1][...] = total.astype(BF16)

    summed = call(sum_kernel, shaped((chunk, 128), BF16))(own_chunk, *got)
    other = along(summed, mirror(2))

    def volume_kernel(own_ref, a_ref, b_ref, matrices, flat_ref, out_ref, features_ref, rows_ref):
        index = lax.axis_index("space")
        odd = index % 2 == 1
        inside = jnp.logical_and(index > 0, index < space - 1)
        got_a, got_b = a_ref[...], b_ref[...]
        got_b = pick(inside, got_b, jnp.zeros_like(got_b))
        values = [pick(odd, got_a, got_b)] + [own_ref[p] for p in range(planes)]
        values.append(pick(odd, got_b, got_a))
        blank = jnp.zeros((channels, depth), BF16)
        begin = pl.multiple_of(lax.axis_index("filt") * brick, brick)
        stacks = {}
        for position, value in enumerate(values):
            rows_ref[position] = jnp.concatenate([blank, value, blank], axis=1)
            cells = rows_ref[position, :, pl.ds(begin, brick + 2 * depth)]
            stacks[position] = stack3(cells, depth)
        results = conv_planes(matrices, stacks, planes, channels, depth)
        for plane in range(planes):
            for row in range(brick_y):
                cells = results[plane][:, (row + 1) * depth : (row + 2) * depth]
                out_ref[:, plane, row, :] = cells.astype(BF16)
        for row in range(low_y):
            features_ref[:, 0, row, :] = flat_ref[:, row * low_depth : (row + 1) * low_depth]

    volume_grad, features = call(
        volume_kernel,
        (
            jax.ShapeDtypeStruct(volume.shape, BF16),
            jax.ShapeDtypeStruct(cotangent.shape, BF16),
        ),
        (pltpu.VMEM((planes + 2, channels, fine_cells + 2 * depth), BF16),),
    )(first_down, halo_a, halo_b, first_back, flat_features)

    final_chunk = call(sum_kernel, shaped((chunk, 128), BF16))(summed, other)
    pieces = [final_chunk] + [along(final_chunk, mirror(4 * k)) for k in range(1, far_side)]

    def join_kernel(*refs):
        high = lax.axis_index("space") // 4
        for k, ref in enumerate(refs[:-1]):
            refs[-1][pl.ds(pl.multiple_of((high ^ k) * chunk, 16), chunk), :] = ref[...]

    group = call(join_kernel, shaped((half, 128), BF16))(*pieces)
    partner = along(group, mirror(1))

    def spread_kernel(mirrored):
        def body(*refs):
            source, (first_out, second_out, first_ref, second_ref, rows_ref, sem) = refs[0], refs[-6:]
            core = lax.axis_index("space") % 2
            rows_ref[...] = source[...].astype(F32)

            def write(rows, near, far, scale):
                unpack(rows_ref, 0, rows, near, scale)
                copy = pltpu.make_async_copy(near, far, sem)
                copy.start()
                copy.wait()

            @pl.when(core == mirrored)
            def _():
                write(first_rows, first_ref, first_out, fine_scale)

            @pl.when(core != mirrored)
            def _():
                write(second_rows, second_ref, second_out, low_scale)

        return body

    first_shape, second_shape = (27, channels, channels), (27, filters, channels)
    results = (jax.ShapeDtypeStruct(first_shape, F32), jax.ShapeDtypeStruct(second_shape, F32))
    scratch = (
        pltpu.VMEM(first_shape, F32),
        pltpu.VMEM(second_shape, F32),
        pltpu.VMEM((half, 128), F32),
        pltpu.SemaphoreType.DMA,
    )
    early = call(spread_kernel(0), results, scratch, out_far=True)(group)
    first_grad, second_grad = call(
        spread_kernel(1), results, scratch, far=(1, 2), aliases={1: 0, 2: 1}, out_far=True
    )(partner, *early)
    return (features, volume_grad, first_grad, second_grad)


def solution(mesh):
    def whole_program(*args):
        return local(mesh.shape["space"], mesh.shape["filt"], *args)

    placed = (
        P(None, "space", "filt", None),
        P(),
        P(None, "filt", None),
        P("filt", "space", None, None),
    )
    return jax.shard_map(
        whole_program,
        mesh=mesh,
        in_specs=placed,
        out_specs=(
            P("filt", "space", None, None),
            P(None, "space", "filt", None),
            P(),
            P(None, "filt", None),
        ),
        check_vma=False,
    )
```

```python
import jax
import jax.numpy as jnp
from jax import lax
from jax.experimental import pallas as pl
from jax.experimental.pallas import tpu as pltpu
from jax.sharding import PartitionSpec as P


F32 = jnp.float32
BF16 = jnp.bfloat16
VMEM_LIMIT = 32 * 1024 * 1024


def call(body, outs, scratch=(), far=(), aliases=None, out_far=False):
    def run(*args):
        kernel = pl.pallas_call(
            body,
            out_shape=outs,
            in_specs=[
                pl.BlockSpec(memory_space=pltpu.HBM if k in far else pltpu.VMEM)
                for k in range(len(args))
            ],
            out_specs=jax.tree.map(
                lambda _: pl.BlockSpec(memory_space=pltpu.HBM if out_far else pltpu.VMEM), outs
            ),
            scratch_shapes=scratch,
            input_output_aliases=aliases or {},
            compiler_params=pltpu.CompilerParams(vmem_limit_bytes=VMEM_LIMIT),
        )
        near = [
            pltpu.with_memory_space_constraint(arg, pltpu.HBM if k in far else pltpu.VMEM)
            for k, arg in enumerate(args)
        ]
        return kernel(*near)

    return run


def shaped(shape, dtype):
    return pltpu.VMEM(shape, dtype)


def dot(lhs, rhs):
    return jnp.dot(lhs, rhs, preferred_element_type=F32)


def dot_cells(lhs, rhs):
    return lax.dot_general(lhs, rhs, (((1,), (1,)), ((), ())), preferred_element_type=F32)


def silu_slope(values):
    part = 1.0 / (1.0 + jnp.exp(-values))
    return part * (1.0 + values * (1.0 - part))


def silu(values):
    return values / (1.0 + jnp.exp(-values))


def stack3(cells, depth):
    count = cells.shape[1]
    lane = lax.broadcasted_iota(jnp.int32, cells.shape, 1) % depth
    wide = cells.astype(F32)
    below = jnp.where(lane == 0, 0.0, pltpu.roll(wide, 1, 1)).astype(BF16)
    above = jnp.where(lane == depth - 1, 0.0, pltpu.roll(wide, count - 1, 1)).astype(BF16)
    return jnp.concatenate([below, cells, above], axis=0)


def shifted_rows(cells, offset, depth):
    if offset == 0:
        return cells
    blank = jnp.zeros((cells.shape[0], depth), cells.dtype)
    if cells.shape[1] == depth:
        return blank
    if offset > 0:
        return jnp.concatenate([cells[:, depth:], blank], axis=1)
    return jnp.concatenate([blank, cells[:, :-depth]], axis=1)


def conv_planes(matrices, stacks, planes, outputs, depth, results=None):
    results = list(results) if results else [None] * planes
    for place, stack in stacks.items():
        first = max(0, place - planes + 1)
        last = min(2, place)
        rows = matrices[first * 3 * outputs : (last + 1) * 3 * outputs, :]
        terms = dot(rows, stack)
        for tap_x in range(first, last + 1):
            for tap_y in range(3):
                begin = ((tap_x - first) * 3 + tap_y) * outputs
                term = shifted_rows(terms[begin : begin + outputs], tap_y - 1, depth)
                target = place - tap_x
                results[target] = term if results[target] is None else results[target] + term
    return results


def weight_planes(grads, stacks, depth):
    planes = len(grads)
    rows = [
        jnp.concatenate([shifted_rows(grad, 1 - tap_y, depth) for tap_y in range(3)], axis=0)
        for grad in grads
    ]
    sums = []
    for tap_x in range(3):
        total = None
        for plane in range(planes):
            term = dot_cells(rows[plane], stacks[plane + tap_x])
            total = term if total is None else total + term
        sums.append(total)
    return sums


def packed(sums, count):
    acc = jnp.concatenate(sums, axis=0)
    rows = acc.shape[0]
    tail = jnp.concatenate([acc[: rows // 2, 128:], acc[rows // 2 :, 128:]], axis=1)
    pieces = [acc[:, :128], tail]
    if count > rows * 3 // 2:
        pieces.append(jnp.zeros((count - rows * 3 // 2, 128), F32))
    return jnp.concatenate(pieces, axis=0)


def unpack(source, base, rows, out, scale):
    half = rows // 2
    outputs = rows // 9
    for pair in range(9):
        main = source[base + pair * outputs : base + (pair + 1) * outputs, :].astype(F32) * scale
        out[3 * pair] = main[:, :64]
        out[3 * pair + 1] = main[:, 64:]
    for piece in range(0, 9 * outputs, 8):
        row = piece if piece < half else piece - half
        tail = source[base + rows + row : base + rows + row + 8, :].astype(F32) * scale
        side = tail[:, :64] if piece < half else tail[:, 64:]
        out[3 * (piece // outputs) + 2, piece % outputs : piece % outputs + 8, :] = side


def forward_matrix(taps, target, outputs):
    for pair in range(9):
        target[pair * outputs : (pair + 1) * outputs, :] = jnp.concatenate(
            [taps[3 * pair + tap_z] for tap_z in range(3)], axis=1
        )


def backward_matrix(taps):
    rows = [
        jnp.concatenate([taps[26 - 3 * pair - tap_z] for pair in range(9)], axis=1)
        for tap_z in range(3)
    ]
    return jnp.concatenate(rows, axis=0).T


def pick(flag, one, other):
    return jnp.where(flag, one, other)


def swap_tables(count):
    ends = [(0, 0), (count - 1, count - 1)]
    table_b = ends + [(i, i + 1) for i in range(1, count - 1, 2)]
    table_b += [(i + 1, i) for i in range(1, count - 1, 2)]
    low = [i for i in range(count - 2) if i % 4 >= 2]
    table_d = [(i, i + 2) for i in low] + [(i + 2, i) for i in low]
    table_d += [(0, 0), (1, 1), (count - 2, count - 2), (count - 1, count - 1)]
    return table_b, table_d


def join_rows(target, place, pieces, brick):
    index = lax.axis_index("filt")
    for slot, piece in enumerate(pieces):
        start = pl.multiple_of((index ^ slot) * brick, brick)
        target[place, :, pl.ds(start, brick)] = piece


def local(space, filt, volume, first_weight, second_weight, cotangent):
    channels, planes, brick_y, depth = volume.shape
    filters = second_weight.shape[1]
    fine_y = brick_y * filt
    low_y = fine_y // 2
    low_depth = depth // 2
    fine_cells = fine_y * depth
    low_cells = low_y * low_depth
    brick = brick_y * depth
    fine_scale = 1.0 / (planes * space * fine_cells) ** 0.5
    low_scale = 1.0 / (planes // 2 * space * low_cells) ** 0.5
    blocks = channels // filters
    extra = low_cells // blocks
    table_b, table_d = swap_tables(space)

    def mirror(mask):
        return [(i, i ^ mask) for i in range(space)]

    def along(piece, table):
        return lax.ppermute(piece, "space", table)

    def across(piece, table, slot):
        pairs = [(i * filt + f, j * filt + (f ^ slot)) for i, j in table for f in range(filt)]
        return lax.ppermute(piece, ("space", "filt"), pairs)


    def message_kernel(*refs):
        far_refs, own_ref, edge_ref, narrow_ref, first_ref = refs[:4], *refs[4:8]
        cells_ref, cot_ref, second_ref, sems = refs[8:]
        odd = lax.axis_index("space") % 2 == 1
        copies = [
            pltpu.make_async_copy(source, target, sems.at[k])
            for k, (source, target) in enumerate(
                zip(far_refs, (cells_ref, cot_ref, second_ref, first_ref))
            )
        ]
        for copy in copies:
            copy.start()
        copies[0].wait()
        for plane in range(planes):
            for row in range(brick_y):
                start = (plane * brick_y + row) * depth
                own_ref[:, start : start + depth] = cells_ref[:, plane, row, :]
        copies[1].wait()
        width = low_y // blocks
        for row in range(low_y):
            block, start = row // width, (row % width) * low_depth
            piece = cot_ref[:, 0, row, :]
            own_ref[
                block * filters : (block + 1) * filters,
                planes * brick + start : planes * brick + start + low_depth,
            ] = piece
        edge_ref[:, :brick] = pick(
            odd, own_ref[:, (planes - 1) * brick : planes * brick], own_ref[:, :brick]
        )
        edge_ref[:, brick:] = own_ref[:, planes * brick :]

        copies[2].wait()
        for tap in range(14):
            narrow_ref[tap] = jnp.concatenate([second_ref[tap], second_ref[tap + 13]], axis=1)
        copies[3].wait()

    own_message, edge_message, narrow, first_taps = call(
        message_kernel,
        (
            shaped((channels, planes * brick + extra), BF16),
            shaped((channels, brick + extra), BF16),
            shaped((14, filters, 128), BF16),
            shaped(first_weight.shape, BF16),
        ),
        (
            pltpu.VMEM(volume.shape, BF16),
            pltpu.VMEM(cotangent.shape, BF16),
            pltpu.VMEM(second_weight.shape, BF16),
            pltpu.SemaphoreType.DMA((4,)),
        ),
        far=(0, 1, 2, 3),
    )(volume, cotangent, second_weight, first_weight)
    own = [own_message] + [across(own_message, mirror(0), slot) for slot in range(1, filt)]
    side_b = [across(edge_message, table_b, slot) for slot in range(filt)]
    side_a = [along(message, mirror(1)) for message in own]

    narrows = [narrow] + [across(narrow, mirror(0), slot) for slot in range(1, filt)]

    def own_kernel(*refs):
        own_refs, taps = refs[:filt], refs[filt]
        fine_ref, sums_ref, matrices, whole_ref = refs[filt + 1 :]
        forward_matrix(taps, matrices, channels)
        for plane in range(planes):
            pieces = [ref[:, plane * brick : (plane + 1) * brick] for ref in own_refs]
            join_rows(whole_ref, plane, pieces, brick)
        stacks = {1 + plane: stack3(whole_ref[plane], depth) for plane in range(planes)}
        for plane in range(planes):
            fine_ref[plane] = stacks[1 + plane]
        sums = conv_planes(matrices, stacks, planes, channels, depth)
        for plane in range(planes):
            sums_ref[plane] = sums[plane]

    own_stacks, own_sums, first_forward = call(
        own_kernel,
        (
            shaped((planes, 3 * channels, fine_cells), BF16),
            shaped((planes, channels, fine_cells), F32),
            shaped((9 * channels, 3 * channels), BF16),
        ),
        (pltpu.VMEM((planes, channels, fine_cells), BF16),),
    )(*own, first_taps)

    def first_kernel(*refs):
        a_refs, b_refs = refs[:filt], refs[filt : 2 * filt]
        sums_ref, matrices, pooled_ref, slope_ref, fine_ref, sides_ref = refs[2 * filt :]
        index = lax.axis_index("space")
        odd = index % 2 == 1
        inside = jnp.logical_and(index > 0, index < space - 1)
        lefts, rights = [], []
        for a_ref, b_ref in zip(a_refs, b_refs):
            got_a = pick(odd, a_ref[:, (planes - 1) * brick : planes * brick], a_ref[:, :brick])
            got_b = b_ref[:, :brick]
            got_b = pick(inside, got_b, jnp.zeros_like(got_b))
            lefts.append(pick(odd, got_a, got_b))
            rights.append(pick(odd, got_b, got_a))
        join_rows(sides_ref, 0, lefts, brick)
        join_rows(sides_ref, 1, rights, brick)
        stacks = {0: stack3(sides_ref[0], depth), planes + 1: stack3(sides_ref[1], depth)}
        fine_ref[0] = stacks[0]
        fine_ref[1] = stacks[planes + 1]
        sums = [sums_ref[plane] for plane in range(planes)]
        pre = conv_planes(matrices, stacks, planes, channels, depth, sums)
        hidden = [silu(value).astype(BF16) for value in pre]
        for plane in range(planes):
            slope_ref[plane] = silu_slope(pre[plane])
        pairs = (
            lax.broadcasted_iota(jnp.int32, (depth, low_depth), 0) // 2
            == lax.broadcasted_iota(jnp.int32, (depth, low_depth), 1)
        ).astype(BF16)
        for row in range(low_y):
            rows = jnp.concatenate(
                [
                    hidden[x][:, (2 * row + y) * depth : (2 * row + y + 1) * depth]
                    for x in range(2)
                    for y in range(2)
                ],
                axis=0,
            )
            sums = dot(rows, pairs)
            total = sums[:channels]
            for piece in range(1, 4):
                total = total + sums[piece * channels : (piece + 1) * channels]
            pooled_ref[:, row * low_depth : (row + 1) * low_depth] = (0.125 * total).astype(BF16)

    pooled, slope, side_stacks = call(
        first_kernel,
        (
            shaped((channels, low_cells), BF16),
            shaped((planes, channels, fine_cells), F32),
            shaped((2, 3 * channels, fine_cells), BF16),
        ),
        (pltpu.VMEM((2, channels, fine_cells), BF16),),
    )(*side_a, *side_b, own_sums, first_forward)

    pool_d = along(pooled, table_d)
    pool_x = along(pooled, mirror(2))
    pool_a = along(pooled, mirror(1))
    pool_ax = along(pool_x, mirror(1))
    pool_ad = along(pool_d, mirror(1))

    def matrix_kernel(*refs):
        forward_ref, back_ref = refs[filt:]
        for slot, ref in enumerate(refs[:filt]):
            values = [ref[t, :, :64] if t < 14 else ref[t - 13, :, 64:] for t in range(27)]
            forward_matrix(values, forward_ref.at[slot], filters)
            back_ref[slot] = backward_matrix(values)

    second_forward, second_back = call(
        matrix_kernel,
        (
            shaped((filt, 9 * filters, 3 * channels), BF16),
            shaped((filt, 9 * channels, 3 * filters), BF16),
        ),
    )(*narrows)

    def back_kernel(taps, out_ref):
        out_ref[...] = backward_matrix([taps[t] for t in range(27)])

    first_back = call(back_kernel, shaped((9 * channels, 3 * channels), BF16))(first_taps)

    first_rows, second_rows = 9 * channels, 9 * filters
    packed_first, packed_second = first_rows * 3 // 2, second_rows * 3 // 2
    far_side = space // 4
    unit = 16 * far_side
    half = -(-max(packed_first, packed_second) // unit) * unit
    chunk = half // far_side
    edge_blocks = fine_cells // 128

    def middle_kernel(*refs):
        own_refs, a_refs, b_refs = refs[:filt], refs[filt : 2 * filt], refs[2 * filt : 3 * filt]
        pool_ref, pa_ref, px_ref, pd_ref, pax_ref, pad_ref = refs[3 * filt : 3 * filt + 6]
        forward_ref, back_ref, slope_ref, own_fine, side_fine = refs[
            3 * filt + 6 : 3 * filt + 11
        ]
        features_ref, down_ref, edge_b_ref, keep_ref, send_ref, parts_ref = refs[3 * filt + 11 :]
        index = lax.axis_index("space")
        odd = index % 2 == 1
        up = (index // 2) % 2 == 1
        inside = jnp.logical_and(index > 0, index < space - 1)
        inside_two = jnp.logical_and(index > 1, index < space - 2)
        blank = jnp.zeros((channels, low_cells), BF16)
        got_d = pick(inside_two, pd_ref[...], blank)
        got_ad = pick(inside_two, pad_ref[...], blank)
        got_a, got_x, got_ax = pa_ref[...], px_ref[...], pax_ref[...]
        other = pick(odd == up, got_ad, got_ax)
        pools = [
            pick(up, got_x, got_d),
            pick(odd, got_a, other),
            pool_ref[...],
            pick(odd, other, got_a),
            pick(up, got_d, got_x),
        ]
        stacks = {k: stack3(value, low_depth) for k, value in enumerate(pools)}

        def cot_of(packed):
            return jnp.concatenate(
                [packed[k * filters : (k + 1) * filters] for k in range(blocks)], axis=1
            ).astype(F32)

        for slot in range(filt):
            pre = conv_planes(forward_ref.at[slot], stacks, 3, filters, low_depth)
            cot_own = cot_of(own_refs[slot][:, planes * brick :])
            cot_a = cot_of(a_refs[slot][:, planes * brick :])
            cot_b = cot_of(b_refs[slot][:, brick:])
            cot_b = pick(inside, cot_b, jnp.zeros_like(cot_b))
            cots = [pick(odd, cot_a, cot_b), cot_own, pick(odd, cot_b, cot_a)]
            downs = [
                (value * silu_slope(pre[plane])).astype(BF16) for plane, value in enumerate(cots)
            ]
            if slot == 0:
                features_ref[...] = silu(pre[1]).astype(BF16)
                second_sums = weight_planes([downs[1]], [stacks[1], stacks[2], stacks[3]], low_depth)
            down_stacks = {k: stack3(value, low_depth) for k, value in enumerate(downs)}
            (part,) = conv_planes(back_ref.at[slot], down_stacks, 1, channels, low_depth)
            parts_ref[lax.axis_index("filt") ^ slot] = part.astype(BF16)

        spread = (
            lax.broadcasted_iota(jnp.int32, (low_depth, depth), 0)
            == lax.broadcasted_iota(jnp.int32, (low_depth, depth), 1) // 2
        ).astype(BF16)
        columns = []
        for row in range(low_y):
            wide = None
            for group in range(filt):
                cells = parts_ref[group, :, row * low_depth : (row + 1) * low_depth]
                term = dot(cells, spread)
                wide = term if wide is None else wide + term
            columns += [0.125 * wide] * 2
        hidden_grad = jnp.concatenate(columns, axis=1)
        grads = [(hidden_grad * slope_ref[p]).astype(BF16) for p in range(planes)]
        for plane in range(planes):
            down_ref[plane] = grads[plane]
        edge_a = pick(odd, grads[0], grads[planes - 1])
        for block in range(edge_blocks):
            start = half + block * channels
            send_ref[start : start + channels, :] = edge_a[:, block * 128 : (block + 1) * 128]
        edge_b_ref[...] = pick(odd, grads[planes - 1], grads[0])
        fine_stacks = [side_fine[0]] + [own_fine[p] for p in range(planes)] + [side_fine[1]]
        first_sums = packed(weight_planes(grads, fine_stacks, depth), half)
        second_sums = packed(second_sums, half)
        keep_ref[...] = pick(odd, second_sums, first_sums)
        send_ref[:half, :] = pick(odd, first_sums, second_sums).astype(BF16)

    flat_features, first_down, edge_b, keep, send = call(
        middle_kernel,
        (
            shaped((filters, low_cells), BF16),
            shaped((planes, channels, fine_cells), BF16),
            shaped((channels, fine_cells), BF16),
            shaped((half, 128), F32),
            shaped((half + edge_blocks * channels, 128), BF16),
        ),
        (
            pltpu.VMEM((filt, channels, low_cells), BF16),
        ),
    )(
        *own,
        *side_a,
        *side_b,
        pooled,
        pool_a,
        pool_x,
        pool_d,
        pool_ax,
        pool_ad,
        second_forward,
        second_back,
        slope,
        own_stacks,
        side_stacks,
    )

    got_core = along(send, mirror(1))

    def split_kernel(keep_ref, got_ref, *refs):
        out_refs, rows_ref = refs[:-1], refs[-1]
        rows_ref[...] = keep_ref[...] + got_ref[:half, :].astype(F32)
        high = lax.axis_index("space") // 4
        out_refs[0][...] = rows_ref[pl.ds(pl.multiple_of(high * chunk, 16), chunk), :]
        for k in range(1, far_side):
            start = pl.multiple_of((high ^ k) * chunk, 16)
            out_refs[k][...] = rows_ref[pl.ds(start, chunk), :].astype(BF16)

    own_chunk, *sends = call(
        split_kernel,
        (shaped((chunk, 128), F32),) + (shaped((chunk, 128), BF16),) * (far_side - 1),
        (pltpu.VMEM((half, 128), F32),),
    )(keep, got_core)
    got = [along(sends[k - 1], mirror(4 * k)) for k in range(1, far_side)]
    halo_a, halo_b = got_core, along(edge_b, table_b)

    def sum_kernel(own_ref, *refs):
        total = own_ref[...].astype(F32)
        for ref in refs[:-1]:
            total = total + ref[...].astype(F32)
        refs[-1][...] = total.astype(BF16)

    summed = call(sum_kernel, shaped((chunk, 128), BF16))(own_chunk, *got)
    other = along(summed, mirror(2))

    def volume_kernel(own_ref, a_ref, b_ref, matrices, flat_ref, out_ref, features_ref, rows_ref):
        index = lax.axis_index("space")
        odd = index % 2 == 1
        inside = jnp.logical_and(index > 0, index < space - 1)
        got_a = jnp.concatenate(
            [
                a_ref[half + k * channels : half + (k + 1) * channels, :]
                for k in range(edge_blocks)
            ],
            axis=1,
        )
        got_b = b_ref[...]
        got_b = pick(inside, got_b, jnp.zeros_like(got_b))
        values = [pick(odd, got_a, got_b)] + [own_ref[p] for p in range(planes)]
        values.append(pick(odd, got_b, got_a))
        blank = jnp.zeros((channels, depth), BF16)
        begin = pl.multiple_of(lax.axis_index("filt") * brick, brick)
        stacks = {}
        for position, value in enumerate(values):
            rows_ref[position] = jnp.concatenate([blank, value, blank], axis=1)
            cells = rows_ref[position, :, pl.ds(begin, brick + 2 * depth)]
            stacks[position] = stack3(cells, depth)
        results = conv_planes(matrices, stacks, planes, channels, depth)
        for plane in range(planes):
            for row in range(brick_y):
                cells = results[plane][:, (row + 1) * depth : (row + 2) * depth]
                out_ref[:, plane, row, :] = cells.astype(BF16)
        for row in range(low_y):
            features_ref[:, 0, row, :] = flat_ref[:, row * low_depth : (row + 1) * low_depth]

    volume_grad, features = call(
        volume_kernel,
        (
            jax.ShapeDtypeStruct(volume.shape, BF16),
            jax.ShapeDtypeStruct(cotangent.shape, BF16),
        ),
        (pltpu.VMEM((planes + 2, channels, fine_cells + 2 * depth), BF16),),
    )(first_down, halo_a, halo_b, first_back, flat_features)

    final_chunk = call(sum_kernel, shaped((chunk, 128), BF16))(summed, other)
    pieces = [final_chunk] + [along(final_chunk, mirror(4 * k)) for k in range(1, far_side)]

    def join_kernel(*refs):
        high = lax.axis_index("space") // 4
        for k, ref in enumerate(refs[:-1]):
            refs[-1][pl.ds(pl.multiple_of((high ^ k) * chunk, 16), chunk), :] = ref[...]

    group = call(join_kernel, shaped((half, 128), BF16))(*pieces)
    partner = along(group, mirror(1))

    def spread_kernel(mirrored):
        def body(*refs):
            source, (first_out, second_out, first_ref, second_ref, rows_ref, sem) = refs[0], refs[-6:]
            core = lax.axis_index("space") % 2
            rows_ref[...] = source[...].astype(F32)

            def write(rows, near, far, scale):
                unpack(rows_ref, 0, rows, near, scale)
                copy = pltpu.make_async_copy(near, far, sem)
                copy.start()
                copy.wait()

            @pl.when(core == mirrored)
            def _():
                write(first_rows, first_ref, first_out, fine_scale)

            @pl.when(core != mirrored)
            def _():
                write(second_rows, second_ref, second_out, low_scale)

        return body

    first_shape, second_shape = (27, channels, channels), (27, filters, channels)
    results = (jax.ShapeDtypeStruct(first_shape, F32), jax.ShapeDtypeStruct(second_shape, F32))
    scratch = (
        pltpu.VMEM(first_shape, F32),
        pltpu.VMEM(second_shape, F32),
        pltpu.VMEM((half, 128), F32),
        pltpu.SemaphoreType.DMA,
    )
    early = call(spread_kernel(0), results, scratch, out_far=True)(group)
    first_grad, second_grad = call(
        spread_kernel(1), results, scratch, far=(1, 2), aliases={1: 0, 2: 1}, out_far=True
    )(partner, *early)
    return (features, volume_grad, first_grad, second_grad)


def solution(mesh):
    def whole_program(*args):
        return local(mesh.shape["space"], mesh.shape["filt"], *args)

    placed = (
        P(None, "space", "filt", None),
        P(),
        P(None, "filt", None),
        P("filt", "space", None, None),
    )
    return jax.shard_map(
        whole_program,
        mesh=mesh,
        in_specs=placed,
        out_specs=(
            P("filt", "space", None, None),
            P(None, "space", "filt", None),
            P(),
            P(None, "filt", None),
        ),
        check_vma=False,
    )
```

```python
import jax
import jax.numpy as jnp
from jax import lax
from jax.experimental import pallas as pl
from jax.experimental.pallas import tpu as pltpu
from jax.sharding import PartitionSpec as P


F32 = jnp.float32
BF16 = jnp.bfloat16
VMEM_LIMIT = 32 * 1024 * 1024


def call(body, outs, scratch=(), far=(), aliases=None, out_far=False):
    def run(*args):
        kernel = pl.pallas_call(
            body,
            out_shape=outs,
            in_specs=[
                pl.BlockSpec(memory_space=pltpu.HBM if k in far else pltpu.VMEM)
                for k in range(len(args))
            ],
            out_specs=jax.tree.map(
                lambda _: pl.BlockSpec(memory_space=pltpu.HBM if out_far else pltpu.VMEM), outs
            ),
            scratch_shapes=scratch,
            input_output_aliases=aliases or {},
            compiler_params=pltpu.CompilerParams(vmem_limit_bytes=VMEM_LIMIT),
        )
        near = [
            pltpu.with_memory_space_constraint(arg, pltpu.HBM if k in far else pltpu.VMEM)
            for k, arg in enumerate(args)
        ]
        return kernel(*near)

    return run


def shaped(shape, dtype):
    return pltpu.VMEM(shape, dtype)


def dot(lhs, rhs):
    return jnp.dot(lhs, rhs, preferred_element_type=F32)


def dot_cells(lhs, rhs):
    return lax.dot_general(lhs, rhs, (((1,), (1,)), ((), ())), preferred_element_type=F32)


def silu_slope(values):
    part = 1.0 / (1.0 + jnp.exp(-values))
    return part * (1.0 + values * (1.0 - part))


def silu(values):
    return values / (1.0 + jnp.exp(-values))


def stack3(cells, depth):
    count = cells.shape[1]
    lane = lax.broadcasted_iota(jnp.int32, cells.shape, 1) % depth
    wide = cells.astype(F32)
    below = jnp.where(lane == 0, 0.0, pltpu.roll(wide, 1, 1)).astype(BF16)
    above = jnp.where(lane == depth - 1, 0.0, pltpu.roll(wide, count - 1, 1)).astype(BF16)
    return jnp.concatenate([below, cells, above], axis=0)


def shifted_rows(cells, offset, depth):
    if offset == 0:
        return cells
    blank = jnp.zeros((cells.shape[0], depth), cells.dtype)
    if cells.shape[1] == depth:
        return blank
    if offset > 0:
        return jnp.concatenate([cells[:, depth:], blank], axis=1)
    return jnp.concatenate([blank, cells[:, :-depth]], axis=1)


def conv_planes(matrices, stacks, planes, outputs, depth, results=None):
    results = list(results) if results else [None] * planes
    for place, stack in stacks.items():
        first = max(0, place - planes + 1)
        last = min(2, place)
        rows = matrices[first * 3 * outputs : (last + 1) * 3 * outputs, :]
        terms = dot(rows, stack)
        for tap_x in range(first, last + 1):
            for tap_y in range(3):
                begin = ((tap_x - first) * 3 + tap_y) * outputs
                term = shifted_rows(terms[begin : begin + outputs], tap_y - 1, depth)
                target = place - tap_x
                results[target] = term if results[target] is None else results[target] + term
    return results


def weight_planes(grads, stacks, depth):
    planes = len(grads)
    rows = [
        jnp.concatenate([shifted_rows(grad, 1 - tap_y, depth) for tap_y in range(3)], axis=0)
        for grad in grads
    ]
    sums = []
    for tap_x in range(3):
        total = None
        for plane in range(planes):
            term = dot_cells(rows[plane], stacks[plane + tap_x])
            total = term if total is None else total + term
        sums.append(total)
    return sums


def packed(sums, count):
    acc = jnp.concatenate(sums, axis=0)
    rows = acc.shape[0]
    tail = jnp.concatenate([acc[: rows // 2, 128:], acc[rows // 2 :, 128:]], axis=1)
    pieces = [acc[:, :128], tail]
    if count > rows * 3 // 2:
        pieces.append(jnp.zeros((count - rows * 3 // 2, 128), F32))
    return jnp.concatenate(pieces, axis=0)


def unpack(source, rows, out, scale, pairs):
    half = rows // 2
    outputs = rows // 9
    for pair in pairs:
        begin = pair * outputs
        main = source[begin : begin + outputs, :].astype(F32) * scale
        out[3 * pair] = main[:, :64]
        out[3 * pair + 1] = main[:, 64:]
        for piece in range(begin, begin + outputs, 8):
            row = rows + (piece if piece < half else piece - half)
            tail = source[row : row + 8, :].astype(F32) * scale
            side = tail[:, :64] if piece < half else tail[:, 64:]
            out[3 * pair + 2, piece - begin : piece - begin + 8, :] = side


def forward_matrix(taps, target, outputs):
    for pair in range(9):
        target[pair * outputs : (pair + 1) * outputs, :] = jnp.concatenate(
            [taps[3 * pair + tap_z] for tap_z in range(3)], axis=1
        )


def backward_matrix(taps):
    rows = [
        jnp.concatenate([taps[26 - 3 * pair - tap_z] for pair in range(9)], axis=1)
        for tap_z in range(3)
    ]
    return jnp.concatenate(rows, axis=0).T


def pick(flag, one, other):
    return jnp.where(flag, one, other)


def swap_tables(count):
    ends = [(0, 0), (count - 1, count - 1)]
    table_b = ends + [(i, i + 1) for i in range(1, count - 1, 2)]
    table_b += [(i + 1, i) for i in range(1, count - 1, 2)]
    low = [i for i in range(count - 2) if i % 4 >= 2]
    table_d = [(i, i + 2) for i in low] + [(i + 2, i) for i in low]
    table_d += [(0, 0), (1, 1), (count - 2, count - 2), (count - 1, count - 1)]
    return table_b, table_d


def join_rows(target, place, pieces, brick):
    index = lax.axis_index("filt")
    for slot, piece in enumerate(pieces):
        start = pl.multiple_of((index ^ slot) * brick, brick)
        target[place, :, pl.ds(start, brick)] = piece


def local(space, filt, volume, first_weight, second_weight, cotangent):
    channels, planes, brick_y, depth = volume.shape
    filters = second_weight.shape[1]
    fine_y = brick_y * filt
    low_y = fine_y // 2
    low_depth = depth // 2
    fine_cells = fine_y * depth
    low_cells = low_y * low_depth
    brick = brick_y * depth
    fine_scale = 1.0 / (planes * space * fine_cells) ** 0.5
    low_scale = 1.0 / (planes // 2 * space * low_cells) ** 0.5
    blocks = channels // filters
    extra = low_cells // blocks
    table_b, table_d = swap_tables(space)

    def mirror(mask):
        return [(i, i ^ mask) for i in range(space)]

    def along(piece, table):
        return lax.ppermute(piece, "space", table)

    def across(piece, table, slot):
        pairs = [(i * filt + f, j * filt + (f ^ slot)) for i, j in table for f in range(filt)]
        return lax.ppermute(piece, ("space", "filt"), pairs)


    def message_kernel(*refs):
        far_refs, own_ref, edge_ref, narrow_ref, first_ref = refs[:4], *refs[4:8]
        cells_ref, cot_ref, second_ref, sems = refs[8:]
        odd = lax.axis_index("space") % 2 == 1
        copies = [
            pltpu.make_async_copy(source, target, sems.at[k])
            for k, (source, target) in enumerate(
                zip(far_refs, (cells_ref, cot_ref, second_ref, first_ref))
            )
        ]
        for copy in copies:
            copy.start()
        copies[0].wait()
        for plane in range(planes):
            for row in range(brick_y):
                start = (plane * brick_y + row) * depth
                own_ref[:, start : start + depth] = cells_ref[:, plane, row, :]
        copies[1].wait()
        width = low_y // blocks
        for row in range(low_y):
            block, start = row // width, (row % width) * low_depth
            piece = cot_ref[:, 0, row, :]
            own_ref[
                block * filters : (block + 1) * filters,
                planes * brick + start : planes * brick + start + low_depth,
            ] = piece
        edge_ref[:, :brick] = pick(
            odd, own_ref[:, (planes - 1) * brick : planes * brick], own_ref[:, :brick]
        )
        edge_ref[:, brick:] = own_ref[:, planes * brick :]

        copies[2].wait()
        for tap in range(14):
            narrow_ref[tap] = jnp.concatenate([second_ref[tap], second_ref[tap + 13]], axis=1)
        copies[3].wait()

    own_message, edge_message, narrow, first_taps = call(
        message_kernel,
        (
            shaped((channels, planes * brick + extra), BF16),
            shaped((channels, brick + extra), BF16),
            shaped((14, filters, 128), BF16),
            shaped(first_weight.shape, BF16),
        ),
        (
            pltpu.VMEM(volume.shape, BF16),
            pltpu.VMEM(cotangent.shape, BF16),
            pltpu.VMEM(second_weight.shape, BF16),
            pltpu.SemaphoreType.DMA((4,)),
        ),
        far=(0, 1, 2, 3),
    )(volume, cotangent, second_weight, first_weight)
    own = [own_message] + [across(own_message, mirror(0), slot) for slot in range(1, filt)]
    side_b = [across(edge_message, table_b, slot) for slot in range(filt)]
    side_a = [along(message, mirror(1)) for message in own]

    narrows = [narrow] + [across(narrow, mirror(0), slot) for slot in range(1, filt)]

    def own_kernel(*refs):
        own_refs, taps = refs[:filt], refs[filt]
        fine_ref, sums_ref, matrices, whole_ref = refs[filt + 1 :]
        forward_matrix(taps, matrices, channels)
        for plane in range(planes):
            pieces = [ref[:, plane * brick : (plane + 1) * brick] for ref in own_refs]
            join_rows(whole_ref, plane, pieces, brick)
        stacks = {1 + plane: stack3(whole_ref[plane], depth) for plane in range(planes)}
        for plane in range(planes):
            fine_ref[plane] = stacks[1 + plane]
        sums = conv_planes(matrices, stacks, planes, channels, depth)
        for plane in range(planes):
            sums_ref[plane] = sums[plane]

    own_stacks, own_sums, first_forward = call(
        own_kernel,
        (
            shaped((planes, 3 * channels, fine_cells), BF16),
            shaped((planes, channels, fine_cells), F32),
            shaped((9 * channels, 3 * channels), BF16),
        ),
        (pltpu.VMEM((planes, channels, fine_cells), BF16),),
    )(*own, first_taps)

    def first_kernel(*refs):
        a_refs, b_refs = refs[:filt], refs[filt : 2 * filt]
        sums_ref, matrices, pooled_ref, slope_ref, fine_ref, sides_ref = refs[2 * filt :]
        index = lax.axis_index("space")
        odd = index % 2 == 1
        inside = jnp.logical_and(index > 0, index < space - 1)
        lefts, rights = [], []
        for a_ref, b_ref in zip(a_refs, b_refs):
            got_a = pick(odd, a_ref[:, (planes - 1) * brick : planes * brick], a_ref[:, :brick])
            got_b = b_ref[:, :brick]
            got_b = pick(inside, got_b, jnp.zeros_like(got_b))
            lefts.append(pick(odd, got_a, got_b))
            rights.append(pick(odd, got_b, got_a))
        join_rows(sides_ref, 0, lefts, brick)
        join_rows(sides_ref, 1, rights, brick)
        stacks = {0: stack3(sides_ref[0], depth), planes + 1: stack3(sides_ref[1], depth)}
        fine_ref[0] = stacks[0]
        fine_ref[1] = stacks[planes + 1]
        sums = [sums_ref[plane] for plane in range(planes)]
        pre = conv_planes(matrices, stacks, planes, channels, depth, sums)
        hidden = [silu(value).astype(BF16) for value in pre]
        for plane in range(planes):
            slope_ref[plane] = silu_slope(pre[plane])
        pairs = (
            lax.broadcasted_iota(jnp.int32, (depth, low_depth), 0) // 2
            == lax.broadcasted_iota(jnp.int32, (depth, low_depth), 1)
        ).astype(BF16)
        for row in range(low_y):
            rows = jnp.concatenate(
                [
                    hidden[x][:, (2 * row + y) * depth : (2 * row + y + 1) * depth]
                    for x in range(2)
                    for y in range(2)
                ],
                axis=0,
            )
            sums = dot(rows, pairs)
            total = sums[:channels]
            for piece in range(1, 4):
                total = total + sums[piece * channels : (piece + 1) * channels]
            pooled_ref[:, row * low_depth : (row + 1) * low_depth] = (0.125 * total).astype(BF16)

    pooled, slope, side_stacks = call(
        first_kernel,
        (
            shaped((channels, low_cells), BF16),
            shaped((planes, channels, fine_cells), F32),
            shaped((2, 3 * channels, fine_cells), BF16),
        ),
        (pltpu.VMEM((2, channels, fine_cells), BF16),),
    )(*side_a, *side_b, own_sums, first_forward)

    pool_d = along(pooled, table_d)
    pool_x = along(pooled, mirror(2))
    pool_a = along(pooled, mirror(1))
    pool_ax = along(pool_x, mirror(1))
    pool_ad = along(pool_d, mirror(1))

    def matrix_kernel(*refs):
        forward_ref, back_ref = refs[filt:]
        for slot, ref in enumerate(refs[:filt]):
            values = [ref[t, :, :64] if t < 14 else ref[t - 13, :, 64:] for t in range(27)]
            forward_matrix(values, forward_ref.at[slot], filters)
            back_ref[slot] = backward_matrix(values)

    second_forward, second_back = call(
        matrix_kernel,
        (
            shaped((filt, 9 * filters, 3 * channels), BF16),
            shaped((filt, 9 * channels, 3 * filters), BF16),
        ),
    )(*narrows)

    def back_kernel(taps, out_ref):
        out_ref[...] = backward_matrix([taps[t] for t in range(27)])

    first_back = call(back_kernel, shaped((9 * channels, 3 * channels), BF16))(first_taps)

    first_rows, second_rows = 9 * channels, 9 * filters
    packed_first, packed_second = first_rows * 3 // 2, second_rows * 3 // 2
    far_side = space // 4
    unit = 16 * far_side
    half = -(-max(packed_first, packed_second) // unit) * unit
    chunk = half // far_side
    edge_blocks = fine_cells // 128

    def middle_kernel(*refs):
        own_refs, a_refs, b_refs = refs[:filt], refs[filt : 2 * filt], refs[2 * filt : 3 * filt]
        pool_ref, pa_ref, px_ref, pd_ref, pax_ref, pad_ref = refs[3 * filt : 3 * filt + 6]
        forward_ref, back_ref, slope_ref, own_fine, side_fine = refs[
            3 * filt + 6 : 3 * filt + 11
        ]
        features_ref, down_ref, edge_b_ref, keep_ref, send_ref, parts_ref = refs[3 * filt + 11 :]
        index = lax.axis_index("space")
        odd = index % 2 == 1
        up = (index // 2) % 2 == 1
        inside = jnp.logical_and(index > 0, index < space - 1)
        inside_two = jnp.logical_and(index > 1, index < space - 2)
        blank = jnp.zeros((channels, low_cells), BF16)
        got_d = pick(inside_two, pd_ref[...], blank)
        got_ad = pick(inside_two, pad_ref[...], blank)
        got_a, got_x, got_ax = pa_ref[...], px_ref[...], pax_ref[...]
        other = pick(odd == up, got_ad, got_ax)
        pools = [
            pick(up, got_x, got_d),
            pick(odd, got_a, other),
            pool_ref[...],
            pick(odd, other, got_a),
            pick(up, got_d, got_x),
        ]
        stacks = {k: stack3(value, low_depth) for k, value in enumerate(pools)}

        def cot_of(packed):
            return jnp.concatenate(
                [packed[k * filters : (k + 1) * filters] for k in range(blocks)], axis=1
            ).astype(F32)

        pres = [
            conv_planes(forward_ref.at[slot], stacks, 3, filters, low_depth)
            for slot in range(filt)
        ]
        all_downs = []
        for slot, pre in enumerate(pres):
            cot_own = cot_of(own_refs[slot][:, planes * brick :])
            cot_a = cot_of(a_refs[slot][:, planes * brick :])
            cot_b = cot_of(b_refs[slot][:, brick:])
            cot_b = pick(inside, cot_b, jnp.zeros_like(cot_b))
            cots = [pick(odd, cot_a, cot_b), cot_own, pick(odd, cot_b, cot_a)]
            all_downs.append(
                [(value * silu_slope(pre[plane])).astype(BF16) for plane, value in enumerate(cots)]
            )
        own_sides = [stacks[1], stacks[2], stacks[3]]
        second_sums = weight_planes([all_downs[0][1]], own_sides, low_depth)
        features_ref[...] = silu(pres[0][1]).astype(BF16)
        for slot, downs in enumerate(all_downs):
            down_stacks = {k: stack3(value, low_depth) for k, value in enumerate(downs)}
            (part,) = conv_planes(back_ref.at[slot], down_stacks, 1, channels, low_depth)
            parts_ref[lax.axis_index("filt") ^ slot] = part.astype(BF16)

        spread = (
            lax.broadcasted_iota(jnp.int32, (low_depth, depth), 0)
            == lax.broadcasted_iota(jnp.int32, (low_depth, depth), 1) // 2
        ).astype(BF16)
        columns = []
        for row in range(low_y):
            wide = None
            for group in range(filt):
                cells = parts_ref[group, :, row * low_depth : (row + 1) * low_depth]
                term = dot(cells, spread)
                wide = term if wide is None else wide + term
            columns += [0.125 * wide] * 2
        hidden_grad = jnp.concatenate(columns, axis=1)
        grads = [(hidden_grad * slope_ref[p]).astype(BF16) for p in range(planes)]
        for plane in range(planes):
            down_ref[plane] = grads[plane]
        edge_a = pick(odd, grads[0], grads[planes - 1])
        for block in range(edge_blocks):
            start = half + block * channels
            send_ref[start : start + channels, :] = edge_a[:, block * 128 : (block + 1) * 128]
        edge_b_ref[...] = pick(odd, grads[planes - 1], grads[0])
        fine_stacks = [side_fine[0]] + [own_fine[p] for p in range(planes)] + [side_fine[1]]
        first_sums = packed(weight_planes(grads, fine_stacks, depth), half)
        second_sums = packed(second_sums, half)
        keep_ref[...] = pick(odd, second_sums, first_sums)
        send_ref[:half, :] = pick(odd, first_sums, second_sums).astype(BF16)

    flat_features, first_down, edge_b, keep, send = call(
        middle_kernel,
        (
            shaped((filters, low_cells), BF16),
            shaped((planes, channels, fine_cells), BF16),
            shaped((channels, fine_cells), BF16),
            shaped((half, 128), F32),
            shaped((half + edge_blocks * channels, 128), BF16),
        ),
        (
            pltpu.VMEM((filt, channels, low_cells), BF16),
        ),
    )(
        *own,
        *side_a,
        *side_b,
        pooled,
        pool_a,
        pool_x,
        pool_d,
        pool_ax,
        pool_ad,
        second_forward,
        second_back,
        slope,
        own_stacks,
        side_stacks,
    )

    got_core = along(send, mirror(1))

    def split_kernel(keep_ref, got_ref, *refs):
        out_refs, rows_ref = refs[:-1], refs[-1]
        rows_ref[...] = keep_ref[...] + got_ref[:half, :].astype(F32)
        high = lax.axis_index("space") // 4
        out_refs[0][...] = rows_ref[pl.ds(pl.multiple_of(high * chunk, 16), chunk), :]
        for k in range(1, far_side):
            start = pl.multiple_of((high ^ k) * chunk, 16)
            out_refs[k][...] = rows_ref[pl.ds(start, chunk), :].astype(BF16)

    own_chunk, *sends = call(
        split_kernel,
        (shaped((chunk, 128), F32),) + (shaped((chunk, 128), BF16),) * (far_side - 1),
        (pltpu.VMEM((half, 128), F32),),
    )(keep, got_core)
    got = [along(sends[k - 1], mirror(4 * k)) for k in range(1, far_side)]
    halo_a, halo_b = got_core, along(edge_b, table_b)

    def sum_kernel(own_ref, *refs):
        total = own_ref[...].astype(F32)
        for ref in refs[:-1]:
            total = total + ref[...].astype(F32)
        refs[-1][...] = total.astype(BF16)

    summed = call(sum_kernel, shaped((chunk, 128), BF16))(own_chunk, *got)
    other = along(summed, mirror(2))

    def volume_kernel(own_ref, a_ref, b_ref, matrices, flat_ref, out_ref, features_ref, rows_ref):
        index = lax.axis_index("space")
        odd = index % 2 == 1
        inside = jnp.logical_and(index > 0, index < space - 1)
        got_a = jnp.concatenate(
            [
                a_ref[half + k * channels : half + (k + 1) * channels, :]
                for k in range(edge_blocks)
            ],
            axis=1,
        )
        got_b = b_ref[...]
        got_b = pick(inside, got_b, jnp.zeros_like(got_b))
        values = [pick(odd, got_a, got_b)] + [own_ref[p] for p in range(planes)]
        values.append(pick(odd, got_b, got_a))
        blank = jnp.zeros((channels, depth), BF16)
        begin = pl.multiple_of(lax.axis_index("filt") * brick, brick)
        stacks = {}
        for position, value in enumerate(values):
            rows_ref[position] = jnp.concatenate([blank, value, blank], axis=1)
            cells = rows_ref[position, :, pl.ds(begin, brick + 2 * depth)]
            stacks[position] = stack3(cells, depth)
        results = conv_planes(matrices, stacks, planes, channels, depth)
        for plane in range(planes):
            for row in range(brick_y):
                cells = results[plane][:, (row + 1) * depth : (row + 2) * depth]
                out_ref[:, plane, row, :] = cells.astype(BF16)
        for row in range(low_y):
            features_ref[:, 0, row, :] = flat_ref[:, row * low_depth : (row + 1) * low_depth]

    volume_grad, features = call(
        volume_kernel,
        (
            jax.ShapeDtypeStruct(volume.shape, BF16),
            jax.ShapeDtypeStruct(cotangent.shape, BF16),
        ),
        (pltpu.VMEM((planes + 2, channels, fine_cells + 2 * depth), BF16),),
    )(first_down, halo_a, halo_b, first_back, flat_features)

    final_chunk = call(sum_kernel, shaped((chunk, 128), BF16))(summed, other)
    pieces = [final_chunk] + [along(final_chunk, mirror(4 * k)) for k in range(1, far_side)]

    def join_kernel(*refs):
        high = lax.axis_index("space") // 4
        for k, ref in enumerate(refs[:-1]):
            refs[-1][pl.ds(pl.multiple_of((high ^ k) * chunk, 16), chunk), :] = ref[...]

    group = call(join_kernel, shaped((half, 128), BF16))(*pieces)
    partner = along(group, mirror(1))

    def spread_kernel(mirrored):
        def body(*refs):
            source, (first_out, second_out, first_ref, second_ref, rows_ref, sem) = refs[0], refs[-6:]
            core = lax.axis_index("space") % 2
            rows_ref[...] = source[...].astype(F32)

            def write(rows, near, far, scale):
                copies = []
                for step in range(3):
                    unpack(rows_ref, rows, near, scale, range(3 * step, 3 * step + 3))
                    taps = pl.ds(9 * step, 9)
                    copies.append(
                        pltpu.make_async_copy(near.at[taps], far.at[taps], sem.at[step])
                    )
                    copies[-1].start()
                for copy in copies:
                    copy.wait()

            @pl.when(core == mirrored)
            def _():
                write(first_rows, first_ref, first_out, fine_scale)

            @pl.when(core != mirrored)
            def _():
                write(second_rows, second_ref, second_out, low_scale)

        return body

    first_shape, second_shape = (27, channels, channels), (27, filters, channels)
    results = (jax.ShapeDtypeStruct(first_shape, F32), jax.ShapeDtypeStruct(second_shape, F32))
    scratch = (
        pltpu.VMEM(first_shape, F32),
        pltpu.VMEM(second_shape, F32),
        pltpu.VMEM((half, 128), F32),
        pltpu.SemaphoreType.DMA((3,)),
    )
    early = call(spread_kernel(0), results, scratch, out_far=True)(group)
    first_grad, second_grad = call(
        spread_kernel(1), results, scratch, far=(1, 2), aliases={1: 0, 2: 1}, out_far=True
    )(partner, *early)
    return (features, volume_grad, first_grad, second_grad)


def solution(mesh):
    def whole_program(*args):
        return local(mesh.shape["space"], mesh.shape["filt"], *args)

    placed = (
        P(None, "space", "filt", None),
        P(),
        P(None, "filt", None),
        P("filt", "space", None, None),
    )
    return jax.shard_map(
        whole_program,
        mesh=mesh,
        in_specs=placed,
        out_specs=(
            P("filt", "space", None, None),
            P(None, "space", "filt", None),
            P(),
            P(None, "filt", None),
        ),
        check_vma=False,
    )
```

```python
import jax
import jax.numpy as jnp
from jax import lax
from jax.experimental import pallas as pl
from jax.experimental.pallas import tpu as pltpu
from jax.sharding import PartitionSpec as P


F32 = jnp.float32
BF16 = jnp.bfloat16
VMEM_LIMIT = 32 * 1024 * 1024


def call(body, outs, scratch=(), far=(), aliases=None, out_far=False):
    def run(*args):
        kernel = pl.pallas_call(
            body,
            out_shape=outs,
            in_specs=[
                pl.BlockSpec(memory_space=pltpu.HBM if k in far else pltpu.VMEM)
                for k in range(len(args))
            ],
            out_specs=jax.tree.map(
                lambda _: pl.BlockSpec(memory_space=pltpu.HBM if out_far else pltpu.VMEM), outs
            ),
            scratch_shapes=scratch,
            input_output_aliases=aliases or {},
            compiler_params=pltpu.CompilerParams(vmem_limit_bytes=VMEM_LIMIT),
        )
        near = [
            pltpu.with_memory_space_constraint(arg, pltpu.HBM if k in far else pltpu.VMEM)
            for k, arg in enumerate(args)
        ]
        return kernel(*near)

    return run


def shaped(shape, dtype):
    return pltpu.VMEM(shape, dtype)


def dot(lhs, rhs):
    return jnp.dot(lhs, rhs, preferred_element_type=F32)


def dot_cells(lhs, rhs):
    return lax.dot_general(lhs, rhs, (((1,), (1,)), ((), ())), preferred_element_type=F32)


def silu_slope(values):
    part = 1.0 / (1.0 + jnp.exp(-values))
    return part * (1.0 + values * (1.0 - part))


def silu(values):
    return values / (1.0 + jnp.exp(-values))


def stack3(cells, depth):
    count = cells.shape[1]
    lane = lax.broadcasted_iota(jnp.int32, cells.shape, 1) % depth
    wide = cells.astype(F32)
    below = jnp.where(lane == 0, 0.0, pltpu.roll(wide, 1, 1)).astype(BF16)
    above = jnp.where(lane == depth - 1, 0.0, pltpu.roll(wide, count - 1, 1)).astype(BF16)
    return jnp.concatenate([below, cells, above], axis=0)


def shifted_rows(cells, offset, depth):
    if offset == 0:
        return cells
    blank = jnp.zeros((cells.shape[0], depth), cells.dtype)
    if cells.shape[1] == depth:
        return blank
    if offset > 0:
        return jnp.concatenate([cells[:, depth:], blank], axis=1)
    return jnp.concatenate([blank, cells[:, :-depth]], axis=1)


def conv_planes(matrices, stacks, planes, outputs, depth, results=None):
    results = list(results) if results else [None] * planes
    for place, stack in stacks.items():
        first = max(0, place - planes + 1)
        last = min(2, place)
        rows = matrices[first * 3 * outputs : (last + 1) * 3 * outputs, :]
        terms = dot(rows, stack)
        for tap_x in range(first, last + 1):
            for tap_y in range(3):
                begin = ((tap_x - first) * 3 + tap_y) * outputs
                term = shifted_rows(terms[begin : begin + outputs], tap_y - 1, depth)
                target = place - tap_x
                results[target] = term if results[target] is None else results[target] + term
    return results


def weight_planes(grads, stacks, depth):
    planes = len(grads)
    rows = [
        jnp.concatenate([shifted_rows(grad, 1 - tap_y, depth) for tap_y in range(3)], axis=0)
        for grad in grads
    ]
    sums = []
    for tap_x in range(3):
        total = None
        for plane in range(planes):
            term = dot_cells(rows[plane], stacks[plane + tap_x])
            total = term if total is None else total + term
        sums.append(total)
    return sums


def packed(sums, count):
    acc = jnp.concatenate(sums, axis=0)
    rows = acc.shape[0]
    tail = jnp.concatenate([acc[: rows // 2, 128:], acc[rows // 2 :, 128:]], axis=1)
    pieces = [acc[:, :128], tail]
    if count > rows * 3 // 2:
        pieces.append(jnp.zeros((count - rows * 3 // 2, 128), F32))
    return jnp.concatenate(pieces, axis=0)


def unpack(source, rows, out, scale, pairs):
    half = rows // 2
    outputs = rows // 9
    for pair in pairs:
        begin = pair * outputs
        main = source[begin : begin + outputs, :].astype(F32) * scale
        out[3 * pair] = main[:, :64]
        out[3 * pair + 1] = main[:, 64:]
        for piece in range(begin, begin + outputs, 8):
            row = rows + (piece if piece < half else piece - half)
            tail = source[row : row + 8, :].astype(F32) * scale
            side = tail[:, :64] if piece < half else tail[:, 64:]
            out[3 * pair + 2, piece - begin : piece - begin + 8, :] = side


def forward_matrix(taps, target, outputs):
    for pair in range(9):
        target[pair * outputs : (pair + 1) * outputs, :] = jnp.concatenate(
            [taps[3 * pair + tap_z] for tap_z in range(3)], axis=1
        )


def backward_matrix(taps):
    rows = [
        jnp.concatenate([taps[26 - 3 * pair - tap_z] for pair in range(9)], axis=1)
        for tap_z in range(3)
    ]
    return jnp.concatenate(rows, axis=0).T


def pick(flag, one, other):
    return jnp.where(flag, one, other)


def swap_tables(count):
    ends = [(0, 0), (count - 1, count - 1)]
    table_b = ends + [(i, i + 1) for i in range(1, count - 1, 2)]
    table_b += [(i + 1, i) for i in range(1, count - 1, 2)]
    low = [i for i in range(count - 2) if i % 4 >= 2]
    table_d = [(i, i + 2) for i in low] + [(i + 2, i) for i in low]
    table_d += [(0, 0), (1, 1), (count - 2, count - 2), (count - 1, count - 1)]
    return table_b, table_d


def join_rows(target, place, pieces, brick):
    index = lax.axis_index("filt")
    for slot, piece in enumerate(pieces):
        start = pl.multiple_of((index ^ slot) * brick, brick)
        target[place, :, pl.ds(start, brick)] = piece


def local(space, filt, volume, first_weight, second_weight, cotangent):
    channels, planes, brick_y, depth = volume.shape
    filters = second_weight.shape[1]
    fine_y = brick_y * filt
    low_y = fine_y // 2
    low_depth = depth // 2
    fine_cells = fine_y * depth
    low_cells = low_y * low_depth
    brick = brick_y * depth
    fine_scale = 1.0 / (planes * space * fine_cells) ** 0.5
    low_scale = 1.0 / (planes // 2 * space * low_cells) ** 0.5
    blocks = channels // filters
    extra = low_cells // blocks
    table_b, table_d = swap_tables(space)

    def mirror(mask):
        return [(i, i ^ mask) for i in range(space)]

    def along(piece, table):
        return lax.ppermute(piece, "space", table)

    def across(piece, table, slot):
        pairs = [(i * filt + f, j * filt + (f ^ slot)) for i, j in table for f in range(filt)]
        return lax.ppermute(piece, ("space", "filt"), pairs)


    def message_kernel(*refs):
        far_refs, own_ref, edge_ref, second_ref, first_ref = refs[:4], *refs[4:8]
        cells_ref, cot_ref, sems = refs[8:]
        odd = lax.axis_index("space") % 2 == 1
        split = channels // 2
        parts = [pl.ds(0, split), pl.ds(split, channels - split)]
        loads = [
            pltpu.make_async_copy(far_refs[0].at[part], cells_ref.at[part], sems.at[4 * k])
            for k, part in enumerate(parts)
        ]
        for load in loads:
            load.start()
        copies = [None] + [
            pltpu.make_async_copy(source, target, sems.at[1 + k])
            for k, (source, target) in enumerate(
                zip(far_refs[1:], (cot_ref, second_ref, first_ref))
            )
        ]
        for copy in copies[1:]:
            copy.start()
        for load, part in zip(loads, parts):
            load.wait()
            for plane in range(planes):
                for row in range(brick_y):
                    start = (plane * brick_y + row) * depth
                    own_ref[part, start : start + depth] = cells_ref[part, plane, row, :]
        copies[1].wait()
        width = low_y // blocks
        for row in range(low_y):
            block, start = row // width, (row % width) * low_depth
            piece = cot_ref[:, 0, row, :]
            own_ref[
                block * filters : (block + 1) * filters,
                planes * brick + start : planes * brick + start + low_depth,
            ] = piece
        edge_ref[:, :brick] = pick(
            odd, own_ref[:, (planes - 1) * brick : planes * brick], own_ref[:, :brick]
        )
        edge_ref[:, brick:] = own_ref[:, planes * brick :]

        copies[2].wait()
        copies[3].wait()

    own_message, edge_message, second_taps, first_taps = call(
        message_kernel,
        (
            shaped((channels, planes * brick + extra), BF16),
            shaped((channels, brick + extra), BF16),
            shaped(second_weight.shape, BF16),
            shaped(first_weight.shape, BF16),
        ),
        (
            pltpu.VMEM(volume.shape, BF16),
            pltpu.VMEM(cotangent.shape, BF16),
            pltpu.SemaphoreType.DMA((5,)),
        ),
        far=(0, 1, 2, 3),
    )(volume, cotangent, second_weight, first_weight)
    own = [own_message] + [across(own_message, mirror(0), slot) for slot in range(1, filt)]
    side_b = [across(edge_message, table_b, slot) for slot in range(filt)]
    side_a = [along(message, mirror(1)) for message in own]

    def narrow_kernel(taps, out_ref):
        for tap in range(14):
            out_ref[tap] = jnp.concatenate([taps[tap], taps[tap + 13]], axis=1)

    narrow = call(narrow_kernel, shaped((14, filters, 128), BF16))(second_taps)
    narrows = [narrow] + [across(narrow, mirror(0), slot) for slot in range(1, filt)]

    def own_kernel(*refs):
        own_refs, taps = refs[:filt], refs[filt]
        fine_ref, sums_ref, matrices, whole_ref = refs[filt + 1 :]
        forward_matrix(taps, matrices, channels)
        for plane in range(planes):
            pieces = [ref[:, plane * brick : (plane + 1) * brick] for ref in own_refs]
            join_rows(whole_ref, plane, pieces, brick)
        stacks = {1 + plane: stack3(whole_ref[plane], depth) for plane in range(planes)}
        for plane in range(planes):
            fine_ref[plane] = stacks[1 + plane]
        sums = conv_planes(matrices, stacks, planes, channels, depth)
        for plane in range(planes):
            sums_ref[plane] = sums[plane]

    own_stacks, own_sums, first_forward = call(
        own_kernel,
        (
            shaped((planes, 3 * channels, fine_cells), BF16),
            shaped((planes, channels, fine_cells), F32),
            shaped((9 * channels, 3 * channels), BF16),
        ),
        (pltpu.VMEM((planes, channels, fine_cells), BF16),),
    )(*own, first_taps)

    def first_kernel(*refs):
        a_refs, b_refs = refs[:filt], refs[filt : 2 * filt]
        sums_ref, matrices, pooled_ref, slope_ref, fine_ref, sides_ref = refs[2 * filt :]
        index = lax.axis_index("space")
        odd = index % 2 == 1
        inside = jnp.logical_and(index > 0, index < space - 1)
        lefts, rights = [], []
        for a_ref, b_ref in zip(a_refs, b_refs):
            got_a = pick(odd, a_ref[:, (planes - 1) * brick : planes * brick], a_ref[:, :brick])
            got_b = b_ref[:, :brick]
            got_b = pick(inside, got_b, jnp.zeros_like(got_b))
            lefts.append(pick(odd, got_a, got_b))
            rights.append(pick(odd, got_b, got_a))
        join_rows(sides_ref, 0, lefts, brick)
        join_rows(sides_ref, 1, rights, brick)
        stacks = {0: stack3(sides_ref[0], depth), planes + 1: stack3(sides_ref[1], depth)}
        fine_ref[0] = stacks[0]
        fine_ref[1] = stacks[planes + 1]
        sums = [sums_ref[plane] for plane in range(planes)]
        pre = conv_planes(matrices, stacks, planes, channels, depth, sums)
        hidden = [silu(value).astype(BF16) for value in pre]
        for plane in range(planes):
            slope_ref[plane] = silu_slope(pre[plane])
        pairs = (
            lax.broadcasted_iota(jnp.int32, (depth, low_depth), 0) // 2
            == lax.broadcasted_iota(jnp.int32, (depth, low_depth), 1)
        ).astype(BF16)
        for row in range(low_y):
            rows = jnp.concatenate(
                [
                    hidden[x][:, (2 * row + y) * depth : (2 * row + y + 1) * depth]
                    for x in range(2)
                    for y in range(2)
                ],
                axis=0,
            )
            sums = dot(rows, pairs)
            total = sums[:channels]
            for piece in range(1, 4):
                total = total + sums[piece * channels : (piece + 1) * channels]
            pooled_ref[:, row * low_depth : (row + 1) * low_depth] = (0.125 * total).astype(BF16)

    pooled, slope, side_stacks = call(
        first_kernel,
        (
            shaped((channels, low_cells), BF16),
            shaped((planes, channels, fine_cells), F32),
            shaped((2, 3 * channels, fine_cells), BF16),
        ),
        (pltpu.VMEM((2, channels, fine_cells), BF16),),
    )(*side_a, *side_b, own_sums, first_forward)

    pool_d = along(pooled, table_d)
    pool_x = along(pooled, mirror(2))
    pool_a = along(pooled, mirror(1))
    pool_ax = along(pool_x, mirror(1))
    pool_ad = along(pool_d, mirror(1))

    def matrix_kernel(*refs):
        forward_ref, back_ref = refs[filt:]
        for slot, ref in enumerate(refs[:filt]):
            values = [ref[t, :, :64] if t < 14 else ref[t - 13, :, 64:] for t in range(27)]
            forward_matrix(values, forward_ref.at[slot], filters)
            back_ref[slot] = backward_matrix(values)

    second_forward, second_back = call(
        matrix_kernel,
        (
            shaped((filt, 9 * filters, 3 * channels), BF16),
            shaped((filt, 9 * channels, 3 * filters), BF16),
        ),
    )(*narrows)

    def back_kernel(taps, out_ref):
        out_ref[...] = backward_matrix([taps[t] for t in range(27)])

    first_back = call(back_kernel, shaped((9 * channels, 3 * channels), BF16))(first_taps)

    first_rows, second_rows = 9 * channels, 9 * filters
    packed_first, packed_second = first_rows * 3 // 2, second_rows * 3 // 2
    far_side = space // 4
    unit = 16 * far_side
    half = -(-max(packed_first, packed_second) // unit) * unit
    chunk = half // far_side
    edge_blocks = fine_cells // 128

    def middle_kernel(*refs):
        own_refs, a_refs, b_refs = refs[:filt], refs[filt : 2 * filt], refs[2 * filt : 3 * filt]
        pool_ref, pa_ref, px_ref, pd_ref, pax_ref, pad_ref = refs[3 * filt : 3 * filt + 6]
        forward_ref, back_ref, slope_ref, own_fine, side_fine = refs[
            3 * filt + 6 : 3 * filt + 11
        ]
        features_ref, down_ref, edge_b_ref, keep_ref, send_ref, parts_ref = refs[3 * filt + 11 :]
        index = lax.axis_index("space")
        odd = index % 2 == 1
        up = (index // 2) % 2 == 1
        inside = jnp.logical_and(index > 0, index < space - 1)
        inside_two = jnp.logical_and(index > 1, index < space - 2)
        blank = jnp.zeros((channels, low_cells), BF16)
        got_d = pick(inside_two, pd_ref[...], blank)
        got_ad = pick(inside_two, pad_ref[...], blank)
        got_a, got_x, got_ax = pa_ref[...], px_ref[...], pax_ref[...]
        other = pick(odd == up, got_ad, got_ax)
        pools = [
            pick(up, got_x, got_d),
            pick(odd, got_a, other),
            pool_ref[...],
            pick(odd, other, got_a),
            pick(up, got_d, got_x),
        ]
        stacks = {k: stack3(value, low_depth) for k, value in enumerate(pools)}

        def cot_of(packed):
            return jnp.concatenate(
                [packed[k * filters : (k + 1) * filters] for k in range(blocks)], axis=1
            ).astype(F32)

        pres = [
            conv_planes(forward_ref.at[slot], stacks, 3, filters, low_depth)
            for slot in range(filt)
        ]
        all_downs = []
        for slot, pre in enumerate(pres):
            cot_own = cot_of(own_refs[slot][:, planes * brick :])
            cot_a = cot_of(a_refs[slot][:, planes * brick :])
            cot_b = cot_of(b_refs[slot][:, brick:])
            cot_b = pick(inside, cot_b, jnp.zeros_like(cot_b))
            cots = [pick(odd, cot_a, cot_b), cot_own, pick(odd, cot_b, cot_a)]
            all_downs.append(
                [(value * silu_slope(pre[plane])).astype(BF16) for plane, value in enumerate(cots)]
            )
        own_sides = [stacks[1], stacks[2], stacks[3]]
        second_sums = weight_planes([all_downs[0][1]], own_sides, low_depth)
        for slot, downs in enumerate(all_downs):
            down_stacks = {k: stack3(value, low_depth) for k, value in enumerate(downs)}
            (part,) = conv_planes(back_ref.at[slot], down_stacks, 1, channels, low_depth)
            parts_ref[lax.axis_index("filt") ^ slot] = part.astype(BF16)

        spread = (
            lax.broadcasted_iota(jnp.int32, (low_depth, depth), 0)
            == lax.broadcasted_iota(jnp.int32, (low_depth, depth), 1) // 2
        ).astype(BF16)
        columns = []
        for row in range(low_y):
            wide = None
            for group in range(filt):
                cells = parts_ref[group, :, row * low_depth : (row + 1) * low_depth]
                term = dot(cells, spread)
                wide = term if wide is None else wide + term
            columns += [0.125 * wide] * 2
        hidden_grad = jnp.concatenate(columns, axis=1)
        grads = [(hidden_grad * slope_ref[p]).astype(BF16) for p in range(planes)]
        for plane in range(planes):
            down_ref[plane] = grads[plane]
        edge_a = pick(odd, grads[0], grads[planes - 1])
        for block in range(edge_blocks):
            start = half + block * channels
            send_ref[start : start + channels, :] = edge_a[:, block * 128 : (block + 1) * 128]
        edge_b_ref[...] = pick(odd, grads[planes - 1], grads[0])
        fine_stacks = [side_fine[0]] + [own_fine[p] for p in range(planes)] + [side_fine[1]]
        first_sums = packed(weight_planes(grads, fine_stacks, depth), half)
        second_sums = packed(second_sums, half)
        features_ref[...] = silu(pres[0][1]).astype(BF16)
        keep_ref[...] = pick(odd, second_sums, first_sums)
        send_ref[:half, :] = pick(odd, first_sums, second_sums).astype(BF16)

    flat_features, first_down, edge_b, keep, send = call(
        middle_kernel,
        (
            shaped((filters, low_cells), BF16),
            shaped((planes, channels, fine_cells), BF16),
            shaped((channels, fine_cells), BF16),
            shaped((half, 128), F32),
            shaped((half + edge_blocks * channels, 128), BF16),
        ),
        (
            pltpu.VMEM((filt, channels, low_cells), BF16),
        ),
    )(
        *own,
        *side_a,
        *side_b,
        pooled,
        pool_a,
        pool_x,
        pool_d,
        pool_ax,
        pool_ad,
        second_forward,
        second_back,
        slope,
        own_stacks,
        side_stacks,
    )

    got_core = along(send, mirror(1))

    def split_kernel(keep_ref, got_ref, *refs):
        out_refs, rows_ref = refs[:-1], refs[-1]
        rows_ref[...] = keep_ref[...] + got_ref[:half, :].astype(F32)
        high = lax.axis_index("space") // 4
        out_refs[0][...] = rows_ref[pl.ds(pl.multiple_of(high * chunk, 16), chunk), :]
        for k in range(1, far_side):
            start = pl.multiple_of((high ^ k) * chunk, 16)
            out_refs[k][...] = rows_ref[pl.ds(start, chunk), :].astype(BF16)

    own_chunk, *sends = call(
        split_kernel,
        (shaped((chunk, 128), F32),) + (shaped((chunk, 128), BF16),) * (far_side - 1),
        (pltpu.VMEM((half, 128), F32),),
    )(keep, got_core)
    got = [along(sends[k - 1], mirror(4 * k)) for k in range(1, far_side)]
    halo_a, halo_b = got_core, along(edge_b, table_b)

    def sum_kernel(own_ref, *refs):
        total = own_ref[...].astype(F32)
        for ref in refs[:-1]:
            total = total + ref[...].astype(F32)
        refs[-1][...] = total.astype(BF16)

    summed = call(sum_kernel, shaped((chunk, 128), BF16))(own_chunk, *got)
    other = along(summed, mirror(2))

    def volume_kernel(own_ref, a_ref, b_ref, matrices, flat_ref, out_ref, features_ref, rows_ref):
        index = lax.axis_index("space")
        odd = index % 2 == 1
        inside = jnp.logical_and(index > 0, index < space - 1)
        got_a = jnp.concatenate(
            [
                a_ref[half + k * channels : half + (k + 1) * channels, :]
                for k in range(edge_blocks)
            ],
            axis=1,
        )
        got_b = b_ref[...]
        got_b = pick(inside, got_b, jnp.zeros_like(got_b))
        values = [pick(odd, got_a, got_b)] + [own_ref[p] for p in range(planes)]
        values.append(pick(odd, got_b, got_a))
        blank = jnp.zeros((channels, depth), BF16)
        begin = pl.multiple_of(lax.axis_index("filt") * brick, brick)
        stacks = {}
        for position, value in enumerate(values):
            rows_ref[position] = jnp.concatenate([blank, value, blank], axis=1)
            cells = rows_ref[position, :, pl.ds(begin, brick + 2 * depth)]
            stacks[position] = stack3(cells, depth)
        results = conv_planes(matrices, stacks, planes, channels, depth)
        for plane in range(planes):
            for row in range(brick_y):
                cells = results[plane][:, (row + 1) * depth : (row + 2) * depth]
                out_ref[:, plane, row, :] = cells.astype(BF16)
        for row in range(low_y):
            features_ref[:, 0, row, :] = flat_ref[:, row * low_depth : (row + 1) * low_depth]

    volume_grad, features = call(
        volume_kernel,
        (
            jax.ShapeDtypeStruct(volume.shape, BF16),
            jax.ShapeDtypeStruct(cotangent.shape, BF16),
        ),
        (pltpu.VMEM((planes + 2, channels, fine_cells + 2 * depth), BF16),),
    )(first_down, halo_a, halo_b, first_back, flat_features)

    final_chunk = call(sum_kernel, shaped((chunk, 128), BF16))(summed, other)
    pieces = [final_chunk] + [along(final_chunk, mirror(4 * k)) for k in range(1, far_side)]

    def join_kernel(*refs):
        high = lax.axis_index("space") // 4
        for k, ref in enumerate(refs[:-1]):
            refs[-1][pl.ds(pl.multiple_of((high ^ k) * chunk, 16), chunk), :] = ref[...]

    group = call(join_kernel, shaped((half, 128), BF16))(*pieces)
    partner = along(group, mirror(1))

    def spread_kernel(mirrored):
        def body(*refs):
            source, (first_out, second_out, first_ref, second_ref, rows_ref, sem) = refs[0], refs[-6:]
            core = lax.axis_index("space") % 2
            rows_ref[...] = source[...].astype(F32)

            def write(rows, near, far, scale):
                copies = []
                for step in range(3):
                    unpack(rows_ref, rows, near, scale, range(3 * step, 3 * step + 3))
                    taps = pl.ds(9 * step, 9)
                    copies.append(
                        pltpu.make_async_copy(near.at[taps], far.at[taps], sem.at[step])
                    )
                    copies[-1].start()
                for copy in copies:
                    copy.wait()

            @pl.when(core == mirrored)
            def _():
                write(first_rows, first_ref, first_out, fine_scale)

            @pl.when(core != mirrored)
            def _():
                write(second_rows, second_ref, second_out, low_scale)

        return body

    first_shape, second_shape = (27, channels, channels), (27, filters, channels)
    results = (jax.ShapeDtypeStruct(first_shape, F32), jax.ShapeDtypeStruct(second_shape, F32))
    scratch = (
        pltpu.VMEM(first_shape, F32),
        pltpu.VMEM(second_shape, F32),
        pltpu.VMEM((half, 128), F32),
        pltpu.SemaphoreType.DMA((3,)),
    )
    early = call(spread_kernel(0), results, scratch, out_far=True)(group)
    first_grad, second_grad = call(
        spread_kernel(1), results, scratch, far=(1, 2), aliases={1: 0, 2: 1}, out_far=True
    )(partner, *early)
    return (features, volume_grad, first_grad, second_grad)


def solution(mesh):
    def whole_program(*args):
        return local(mesh.shape["space"], mesh.shape["filt"], *args)

    placed = (
        P(None, "space", "filt", None),
        P(),
        P(None, "filt", None),
        P("filt", "space", None, None),
    )
    return jax.shard_map(
        whole_program,
        mesh=mesh,
        in_specs=placed,
        out_specs=(
            P("filt", "space", None, None),
            P(None, "space", "filt", None),
            P(),
            P(None, "filt", None),
        ),
        check_vma=False,
    )
```
